32 devices in a mesh: hor: 4 (over y, core), lat: 8 (over z, x).
Axes of the slice: x: 2, y: 2, z: 4, core: 2. Of those that a mesh axis runs over, the one named last changes fastest.
Arguments:
- window: float32 [4, 69, 64, 128], P('hor', None, 'lat'), may hold values from -6 to 6
- fresh_noise: float32 [69, 64, 128], P(None, 'lat'), may hold values from -6 to 6
- level_index: int32 [4], P('hor'), may hold values from 4 to 63
- plan: float32 [64], replicated, may hold values from 0.07 to 38.42, as said below
- retention: float32 [4, 192], P('hor'), may hold values from 0.12 to 1
- lift_weight: bfloat16 [192, 69], replicated, may hold values from -0.75 to 0.75
- mod_scale: float32 [192], replicated, may hold values from -3 to 3
- mod_shift: float32 [192], replicated, may hold values from -3 to 3
- conv_weight: bfloat16 [3, 192, 576], replicated, may hold values from -0.15625 to 0.15625
- out_weight: bfloat16 [69, 192], replicated, may hold values from -0.4375 to 0.4375
Outputs:
- window_out: float32 [4, 69, 64, 128], P('hor', None, 'lat')
- rolled: float32 [4, 69, 64, 128], P('hor', None, 'lat')
The draws below stay inside these ranges and needn't reach their ends.
Inputs may be any that keep to these rules, and one draw needn't show every extreme that they name: `plan`: rising from each entry to the next.
All inputs are finite; a program needn't handle non-finite values.
Results may differ from the reference program's by a relative error of at most 0.00064.
Values may be sent and summed in bfloat16 or wider, within the bound.
A program may use at most 64 MiB of HBM per device.

```python
import jax
import jax.numpy as jnp
from jax import lax

C = 69
HIDDEN_CHANNELS = 192
LON = 128
POOL = 4
STEPS = 3
LEVELS = 64
LEAD_FRAMES = 4
LAT = 64


def draw_level_index(key, part):
    span_size = max(1, (LEVELS - STEPS - 2) // LEAD_FRAMES)
    base_level = STEPS + 1 + jnp.arange(LEAD_FRAMES, dtype=jnp.int32) * (LEVELS - STEPS - 2) // LEAD_FRAMES
    offsets = jax.random.randint(jax.random.fold_in(key, 3), (LEAD_FRAMES,), 0, span_size, dtype=jnp.int32)
    levels = jnp.minimum(base_level + offsets, LEVELS - 1)
    levels = levels.at[0].set(STEPS + 1).at[LEAD_FRAMES - 1].set(LEVELS - 1)
    return levels.astype(jnp.int32)


def draw_plan(key, part):
    key_inc = jax.random.fold_in(key, 5)
    steps_up = jax.random.uniform(key_inc, (LEVELS,), jnp.float32, 0.05, 0.6)
    return (0.02 + jnp.cumsum(steps_up)).astype(jnp.float32)


def draw_retention(key, part):
    key_mask = jax.random.fold_in(key, 7)
    key_fast = jax.random.fold_in(key, 8)
    key_slow = jax.random.fold_in(key, 9)
    spike_key = jax.random.fold_in(key, 10)
    depth_key = jax.random.fold_in(key, 12)
    slow_share = 0.5
    slow_mask = jax.random.uniform(key_mask, (HIDDEN_CHANNELS,)) < slow_share
    fast_rate = jax.random.uniform(key_fast, (LEAD_FRAMES, HIDDEN_CHANNELS), jnp.float32, 0.25, 0.6)
    slow_rate = 1.0 - jax.random.uniform(key_slow, (LEAD_FRAMES, HIDDEN_CHANNELS), jnp.float32, 0.2, 1.0) / LEAD_FRAMES
    baseline_rate = jnp.where(slow_mask[None, :], slow_rate, fast_rate)
    spike_frames = jax.random.randint(spike_key, (2,), 0, LEAD_FRAMES, dtype=jnp.int32)
    struck_frame = jnp.any(jnp.arange(LEAD_FRAMES, dtype=jnp.int32)[:, None] == spike_frames[None, :], axis=1)
    spike_depth = jax.random.uniform(depth_key, (HIDDEN_CHANNELS,), jnp.float32, 0.5, 0.8)
    frame_rates = jnp.where(struck_frame[:, None], baseline_rate * spike_depth[None, :], baseline_rate)
    return frame_rates.astype(jnp.float32)


def block_levels(own_key, shape, pieces, low, high):
    def one(dim, blocks):
        heights = jax.random.uniform(jax.random.fold_in(jax.random.fold_in(own_key, 6), dim), (blocks,), jnp.float32, low / len(pieces), high / len(pieces))
        return jnp.repeat(jnp.exp(heights), shape[dim] // blocks).reshape((-1,) + (1,) * (len(shape) - dim - 1))

    gain = one(*pieces[0])
    for cut in pieces[1:]:
        gain = gain * one(*cut)
    return gain


def scatter_about(stream_key, shape, scale, limit, cuts=(), kind=jnp.bfloat16):
    gain = block_levels(stream_key, shape, cuts, -0.22, 0.18) if cuts else 1.0
    array = jax.random.normal(stream_key, shape, jnp.float32) * scale * gain
    return jnp.minimum(jnp.maximum(array, -limit), limit).astype(kind)


def setup_inputs(seed: int = 0) -> dict:
    seeds = jax.random.split(jax.random.key(seed), 11)
    window = scatter_about(seeds[0], (LEAD_FRAMES, C, LAT, LON), 1.0, 6.0, ((0, 4), (2, 8)), jnp.float32)
    fresh_noise = scatter_about(seeds[1], (C, LAT, LON), 1.0, 6.0, ((1, 8),), jnp.float32)
    level_index = draw_level_index(jax.random.fold_in(seeds[10], 71), 0)
    plan = draw_plan(jax.random.fold_in(seeds[10], 71), 0)
    retention = draw_retention(jax.random.fold_in(seeds[10], 71), 0)
    lift_weight = scatter_about(seeds[5], (HIDDEN_CHANNELS, C), C ** -0.5, 0.75)
    mod_scale = scatter_about(seeds[6], (HIDDEN_CHANNELS,), 0.3, 3.0, (), jnp.float32)
    mod_shift = scatter_about(seeds[7], (HIDDEN_CHANNELS,), 0.5, 3.0, (), jnp.float32)
    conv_weight = scatter_about(seeds[8], (3, HIDDEN_CHANNELS, 3 * HIDDEN_CHANNELS), (9 * HIDDEN_CHANNELS) ** -0.5, 0.15625)
    out_weight = scatter_about(seeds[9], (C, HIDDEN_CHANNELS), HIDDEN_CHANNELS ** -0.5, 0.4375)
    return dict(window=window, fresh_noise=fresh_noise, level_index=level_index, plan=plan, retention=retention, lift_weight=lift_weight, mod_scale=mod_scale, mod_shift=mod_shift, conv_weight=conv_weight, out_weight=out_weight)


def lookup(sched_table, level_at):
    levels = jnp.arange(sched_table.shape[0], dtype=jnp.int32)
    onehot = (level_at[:, None] == levels[None, :]).astype(jnp.float32)
    return lax.optimization_barrier(jnp.sum(onehot * sched_table[None, :], axis=1))

def lift_frame(frame_in, scale_mod, shift_mod, lift_weight):
    lifted = jnp.einsum('dc,clw->dlw', lift_weight.astype(jnp.float32), frame_in.astype(jnp.float32))
    return jax.nn.silu(lifted * scale_mod[:, None, None] + shift_mod[:, None, None]).astype(jnp.bfloat16)

def pool_cells(features):
    hidden, lat_rows, lon_cells = features.shape
    blocks = features.astype(jnp.float32).reshape(hidden, lat_rows // POOL, POOL, lon_cells // POOL, POOL)
    return lax.optimization_barrier(jnp.mean(blocks, axis=(2, 4))).reshape(hidden, -1)

def upsample(context, lat_rows, lon_cells):
    hidden = context.shape[0]
    coarse = context.reshape(hidden, lat_rows // POOL, 1, lon_cells // POOL, 1)
    spread_ctx = jnp.broadcast_to(coarse, (hidden, lat_rows // POOL, POOL, lon_cells // POOL, POOL))
    return spread_ctx.reshape(hidden, lat_rows, lon_cells)

def conv_frame(features, conv_weight):
    lat_rows = features.shape[1]
    padded = jnp.pad(features, ((0, 0), (1, 1), (0, 0)))
    conv_sum = jnp.zeros((conv_weight.shape[1],) + features.shape[1:], jnp.float32)
    for row_off in range(3):
        row_slab = padded[:, row_off:row_off + lat_rows, :]
        stacked = jnp.concatenate([jnp.roll(row_slab, 1 - col_off, axis=2) for col_off in range(3)], axis=0)
        conv_sum = conv_sum + jnp.einsum('dk,klw->dlw', conv_weight[row_off].astype(jnp.float32), stacked.astype(jnp.float32))
    return conv_sum

def finish_frame(features, context, conv_weight, out_weight):
    conv_sum = conv_frame(features, conv_weight)
    mixed_sum = features.astype(jnp.float32) + conv_sum + upsample(context, features.shape[1], features.shape[2])
    gated_out = jax.nn.silu(mixed_sum).astype(jnp.bfloat16)
    return jnp.einsum('cd,dlw->clw', out_weight.astype(jnp.float32), gated_out.astype(jnp.float32))

def reference(window, fresh_noise, level_index, plan, retention, lift_weight, mod_scale, mod_shift, conv_weight, out_weight):
    current = window
    for section in range(STEPS):
        sigma_now = lookup(plan, level_index - section)
        sigma_next = lookup(plan, level_index - section - 1)
        in_scale = 1.0 / jnp.sqrt(sigma_now * sigma_now + 1.0)
        scaled = (current * in_scale[:, None, None, None]).astype(jnp.bfloat16)
        log_sigma = jnp.log(sigma_now)
        scale_mod = 1.0 + log_sigma[:, None] * mod_scale[None, :]
        shift_mod = log_sigma[:, None] * mod_shift[None, :]
        features = lax.map(lambda packed: lift_frame(packed[0], packed[1], packed[2], lift_weight), (scaled, scale_mod, shift_mod))
        pooled = lax.map(pool_cells, features)

        def carry_step(running, packed):
            running = packed[0][:, None] * running + packed[1]
            return (running, running)
        _, context = lax.scan(carry_step, jnp.zeros(pooled.shape[1:], jnp.float32), (retention, pooled))
        outputs = lax.map(lambda packed: finish_frame(packed[0], packed[1], conv_weight, out_weight), (features, context))
        skip_scale = 1.0 / (sigma_now * sigma_now + 1.0)
        out_scale = sigma_now * in_scale
        denoised = skip_scale[:, None, None, None] * current + out_scale[:, None, None, None] * outputs
        current = denoised + (sigma_next / sigma_now)[:, None, None, None] * (current - denoised)
    top_sigma = plan[LEVELS - 1]
    rolled = jnp.concatenate([current[1:], (top_sigma * fresh_noise)[None]], axis=0)
    return (current, rolled)
```

```python
import functools

import jax
import jax.numpy as jnp
from jax import lax
from jax.experimental import pallas as pl
from jax.experimental.pallas import tpu as pltpu
from jax.sharding import PartitionSpec as P

POOL = 4
STEPS = 3
MESH = pl.DeviceIdType.MESH
F32 = jnp.float32
BF16 = jnp.bfloat16
WIRE = jnp.bfloat16


def dot(a, b):
    return jnp.dot(a, b, preferred_element_type=F32)


def kernel(
    rows,
    lon,
    n_hor,
    n_lat,
    lvl_h,
    plan_h,
    win_h,
    fresh_h,
    ret_h,
    msc_h,
    msh_h,
    lift_h,
    convw_h,
    outw_h,
    wout,
    arr,
    lvl,
    plan,
    win,
    ret,
    msc,
    msh,
    liftt,
    convw,
    outw,
    liftw,
    taps,
    base_send,
    base_recv,
    rest_send,
    rest_recv,
    cur,
    stack,
    acc,
    up,
    coef,
    mods,
    smsh,
    poolm,
    spread,
    ctx,
    hsend,
    hrecv,
    psend,
    precv,
    rrecv,
    h_ssem,
    h_rsem,
    p_ssem,
    p_rsem,
    r_ssem,
    r_rsem,
    l_sem,
    f_sem,
):
    hidden, chans = liftw.shape
    half = hidden // 2
    n_pairs = rows // 2
    hor = lax.axis_index("hor")
    lat = lax.axis_index("lat")

    barrier = pltpu.get_barrier_semaphore()

    @pl.when(lat > 0)
    def _():
        pl.semaphore_signal(barrier, inc=1, device_id={"lat": lat - 1}, device_id_type=MESH)

    @pl.when(lat < n_lat - 1)
    def _():
        pl.semaphore_signal(barrier, inc=1, device_id={"lat": lat + 1}, device_id_type=MESH)

    for d in range(1, n_hor):
        pl.semaphore_signal(
            barrier, inc=1, device_id={"hor": lax.rem(hor + d, n_hor)}, device_id_type=MESH
        )

    pairs = [(win_h, win), (lvl_h, lvl), (plan_h, plan)]
    pairs += [(msc_h, msc), (msh_h, msh), (ret_h, ret), (lift_h, liftt)]
    pairs += [(convw_h, convw), (outw_h, outw)]
    loads = [pltpu.make_async_copy(a, b, l_sem.at[i]) for i, (a, b) in enumerate(pairs)]
    fresh_load = pltpu.make_async_copy(fresh_h, arr, l_sem.at[len(pairs)])
    for load in loads:
        load.start()

    @pl.when(hor == n_hor - 1)
    def _():
        fresh_load.start()

    def has(side):
        low, high = lat > 0, lat < n_lat - 1
        if isinstance(side, int):
            return low if side == 0 else high
        return jnp.logical_or(
            jnp.logical_and(side == 0, low), jnp.logical_and(side == 1, high)
        )

    for side in range(2):

        @pl.when(jnp.logical_not(has(side)))
        def _():
            hrecv[:, side] = jnp.zeros_like(hrecv[:, side])

    stack[0] = jnp.zeros_like(stack[0])
    stack[rows + 1] = jnp.zeros_like(stack[rows + 1])

    def column(row_ref_value, start, count):
        sub = lax.broadcasted_iota(jnp.int32, (count, hidden), 0) + start
        lane = lax.broadcasted_iota(jnp.int32, (count, hidden), 1)
        return jnp.sum(jnp.where(sub == lane, row_ref_value, 0.0), axis=1, keepdims=True)

    def packed_rate(value):
        lane = lax.broadcasted_iota(jnp.int32, (half, lon), 1)
        lo = jnp.broadcast_to(column(value, 0, half), (half, lon))
        hi = jnp.broadcast_to(column(value, half, half), (half, lon))
        return jnp.where(lane < lon // 2, lo, hi)

    groups = lon // POOL
    k = lax.broadcasted_iota(jnp.int32, (rows * lon, lon), 0)
    n = lax.broadcasted_iota(jnp.int32, (rows * lon, lon), 1)
    shift = POOL.bit_length() - 1
    row_of = lax.shift_right_logical(k, lon.bit_length() - 1)
    want = lax.shift_right_logical(row_of, shift) * groups + lax.shift_right_logical(
        lax.bitwise_and(k, lon - 1), shift
    )
    poolm[...] = jnp.where(want == n, 1.0 / (POOL * POOL), 0.0).astype(BF16)
    for side in range(2):
        k = lax.broadcasted_iota(jnp.int32, (2 * lon, 2 * lon), 0)
        n = lax.broadcasted_iota(jnp.int32, (2 * lon, 2 * lon), 1)
        want = side * (lon // 2) + lax.shift_right_logical(n, shift)
        spread[side] = jnp.where(lax.bitwise_and(k, lon - 1) == want, 1.0, 0.0).astype(BF16)

    def sigma(s, width):
        at = lvl[0] - s
        now = jnp.full((1, width), plan[jnp.maximum(at, 0)], F32)
        after = jnp.full((1, width), plan[jnp.maximum(at - 1, 0)], F32)
        return now, after

    def in_scale_of(now):
        return 1.0 / jnp.sqrt(now * now + 1.0)

    def halo_copy(s, side):
        return pltpu.make_async_remote_copy(
            src_ref=hsend.at[s, side],
            dst_ref=hrecv.at[s, 1 - side],
            send_sem=h_ssem.at[s, side],
            recv_sem=h_rsem.at[s, 1 - side],
            device_id={"lat": lat - 1 + 2 * side},
            device_id_type=MESH,
        )

    def send_halo(s, side):
        @pl.when(has(side))
        def _():
            halo_copy(s, side).start()

    back = {"hor": hor - 1}
    base_copy = pltpu.make_async_remote_copy(
        src_ref=base_send,
        dst_ref=base_recv,
        send_sem=f_sem.at[0],
        recv_sem=f_sem.at[1],
        device_id=back,
        device_id_type=MESH,
    )

    def rest_copy(u):
        part = pl.ds(0 if u == 0 else rows - 1 if u == 1 else 1, 1 if u < 2 else rows - 2)
        return pltpu.make_async_remote_copy(
            src_ref=rest_send.at[part],
            dst_ref=rest_recv.at[part],
            send_sem=f_sem.at[2 + u],
            recv_sem=f_sem.at[5 + u],
            device_id=back,
            device_id_type=MESH,
        )

    def pool_copy(s, d):
        return pltpu.make_async_remote_copy(
            src_ref=psend.at[s],
            dst_ref=precv.at[s, d - 1],
            send_sem=p_ssem.at[s, d - 1],
            recv_sem=p_rsem.at[s, d - 1],
            device_id={"hor": hor + d},
            device_id_type=MESH,
        )

    def rate_copy(d):
        return pltpu.make_async_remote_copy(
            src_ref=ret,
            dst_ref=rrecv.at[d - 1],
            send_sem=r_ssem.at[d - 1],
            recv_sem=r_rsem.at[d - 1],
            device_id={"hor": hor + d},
            device_id_type=MESH,
        )

    def half_silu(h):
        return h + h * jnp.tanh(h)

    def wide(ref, first):
        return jnp.concatenate([ref[first], ref[first + 1]], axis=1)

    def shifted(feat):
        low = feat.astype(BF16)
        ahead = pltpu.roll(feat, 1, 1).astype(BF16)
        behind = pltpu.roll(feat, lon - 1, 1).astype(BF16)
        return ahead, low, behind

    def place(feat, block):
        for b, part in enumerate(shifted(feat)):
            stack[block, b * hidden : (b + 1) * hidden, :] = part

    for load in loads[0:3]:
        load.wait()
    scale = in_scale_of(sigma(0, lon)[0])
    for side, row in enumerate((0, rows - 1)):
        edge_row = win[pl.ds(row, chans, stride=rows), :]
        hsend[0, side, 0:chans, :] = (edge_row * scale).astype(BF16)
    n_near = jnp.where(lat > 0, 1, 0) + jnp.where(lat < n_lat - 1, 1, 0)
    pl.semaphore_wait(barrier, n_near + (n_hor - 1))
    for side in range(2):
        send_halo(0, side)
    for load in loads[3:7]:
        load.wait()
    for d in range(1, n_hor):

        @pl.when(hor + d < n_hor)
        def _():
            rate_copy(d).start()

    for row in range(rows):
        cur[row] = win[pl.ds(row, chans, stride=rows), :]
    mods[0] = jnp.broadcast_to(column(msc[...], 0, hidden), (hidden, lon))
    mods[1] = jnp.broadcast_to(column(msh[...], 0, hidden), (hidden, lon))
    eye = (
        lax.broadcasted_iota(jnp.int32, (chans, chans), 0)
        == lax.broadcasted_iota(jnp.int32, (chans, chans), 1)
    ).astype(F32).astype(BF16)
    liftw[...] = lax.dot_general(
        liftt[...], eye, (((0,), (0,)), ((), ())), preferred_element_type=F32
    ).astype(BF16)

    for load in loads[7:]:
        load.wait()
    taps[...] = jnp.concatenate([convw[a] for a in range(3)], axis=1)

    @pl.loop(0, STEPS)
    def _(s):
        now, after = sigma(s, lon)
        scale = in_scale_of(now)
        log_sigma = jnp.log(now)
        ratio = after / now
        keep = ratio + (1.0 - ratio) / (now * now + 1.0)
        gain = (1.0 - ratio) * (now * scale)
        scale_next = in_scale_of(after)

        @pl.when((s == STEPS - 1) & (hor > 0))
        def _():
            for row in range(rows):
                base_send[row, 0:chans, :] = (keep * cur[row]).astype(BF16)
            base_copy.start()

        smsh[0] = 0.5 * (1.0 + log_sigma * mods[0])
        smsh[1] = 0.5 * (log_sigma * mods[1])
        for p in range(n_pairs):
            scaled = jnp.concatenate(
                [(cur[2 * p + i] * scale).astype(BF16) for i in range(2)], axis=1
            )
            lifted = dot(liftw[...], scaled)
            for i in range(2):
                h = lifted[:, i * lon : (i + 1) * lon] * smsh[0] + smsh[1]
                place(half_silu(h), 2 * p + i + 1)
        flat = jnp.concatenate(
            [stack[row + 1, hidden : 2 * hidden, :] for row in range(rows)], axis=1
        )
        pooled = dot(flat, poolm[...])
        pooled = pooled[0:half] + pltpu.roll(pooled[half:hidden], lon // 2, 1)
        psend[s] = pooled.astype(WIRE)
        for d in range(1, n_hor):

            @pl.when(hor + d < n_hor)
            def _():
                pool_copy(s, d).start()

        ctx[...] = pooled
        for p in range(n_pairs):
            rhs = jnp.concatenate([wide(stack, 2 * p + a) for a in range(3)], axis=0)
            total = dot(taps[...], rhs)
            for i in range(2):
                acc[2 * p + i] = total[:, i * lon : (i + 1) * lon]

        @pl.when(s == 0)
        def _():
            coef[0] = packed_rate(ret[...])
            for d in range(1, n_hor):

                @pl.when(hor >= d)
                def _():
                    rate_copy(d).wait_recv()
                    if d < n_hor - 1:
                        coef[d] = coef[d - 1] * packed_rate(rrecv[d - 1])

        for d in range(1, n_hor):

            @pl.when(hor >= d)
            def _():
                pool_copy(s, d).wait_recv()
                ctx[...] += coef[d - 1] * precv[s, d - 1].astype(F32)

        total = ctx[...]
        high = total.astype(BF16)
        low = (total - high.astype(F32)).astype(BF16)
        both = jnp.concatenate([high, low], axis=1)
        for side in range(2):
            spread_up = dot(both, spread[side])
            for tok in range(2):
                up[tok, side * half : (side + 1) * half, :] = spread_up[:, tok * lon : (tok + 1) * lon]

        def gate(row, extra, tok):
            feat = stack[row + 1, hidden : 2 * hidden, :].astype(F32)
            h = 0.5 * (feat + extra + up[tok])
            return half_silu(h).astype(BF16)

        def advance(row, outputs):
            nxt = keep * cur[row] + gain * outputs
            cur[row] = nxt
            rest_send[row, 0:chans, :] = (nxt - base_send[row, 0:chans, :].astype(F32)).astype(BF16)
            return nxt

        def finish_inner():
            for first in range(1, rows - 1, 2):
                gated = jnp.concatenate(
                    [gate(row, acc[row], row // POOL) for row in (first, first + 1)], axis=1
                )
                outputs = dot(outw[...], gated)
                for i in range(2):
                    advance(first + i, outputs[:, i * lon : (i + 1) * lon])

            @pl.when((s == STEPS - 1) & (hor > 0))
            def _():
                rest_copy(2).start()

        early = (hor < 2) | (s == STEPS - 1)

        @pl.when(early)
        def _():
            finish_inner()

        def wait_edges():
            for side in range(2):

                @pl.when(has(side))
                def _():
                    halo_copy(s, 1 - side).wait_recv()

        def finish_edges():
            near = jnp.concatenate([hrecv[s, side, 0:chans, :] for side in range(2)], axis=1)
            near = dot(liftw[...], near)
            gated = []
            for side, row in enumerate((0, rows - 1)):
                h = near[:, side * lon : (side + 1) * lon] * smsh[0] + smsh[1]
                feat = jnp.where(has(side), half_silu(h), 0.0)
                extra = acc[row] + dot(convw[2 * side], jnp.concatenate(shifted(feat), axis=0))
                gated.append(gate(row, extra, row // POOL))
            outputs = dot(outw[...], jnp.concatenate(gated, axis=1))
            later = s + 1
            for side, row in enumerate((0, rows - 1)):
                nxt = advance(row, outputs[:, side * lon : (side + 1) * lon])
                hsend[later, side, 0:chans, :] = (nxt * scale_next).astype(BF16)

        def send_edges():
            for side in range(2):

                @pl.when((s < STEPS - 1) & has(side))
                def _():
                    halo_copy(s + 1, side).start()

        wait_edges()
        finish_edges()
        send_edges()

        @pl.when((s == STEPS - 1) & (hor > 0))
        def _():
            for u in range(2):
                rest_copy(u).start()

        @pl.when(jnp.logical_not(early))
        def _():
            finish_inner()

    for row in range(rows):
        wout[pl.ds(row, chans, stride=rows), :] = cur[row]

    @pl.when(hor == n_hor - 1)
    def _():
        fresh_load.wait()
        arr[...] = plan[plan.shape[0] - 1] * arr[...]

    @pl.when(hor < n_hor - 1)
    def _():
        base_copy.wait_recv()
        for u, unit in ((2, range(1, rows - 1)), (0, [0]), (1, [rows - 1])):
            rest_copy(u).wait_recv()
            for row in unit:
                arr[pl.ds(row, chans, stride=rows), :] = base_recv[row, 0:chans, :].astype(
                    F32
                ) + rest_recv[row, 0:chans, :].astype(F32)

    for d in range(1, n_hor):

        @pl.when(hor + d < n_hor)
        def _():
            rate_copy(d).wait_send()
            for s in range(STEPS):
                pool_copy(s, d).wait_send()

    for s in range(STEPS):
        for side in range(2):

            @pl.when(has(side))
            def _():
                halo_copy(s, side).wait_send()

    @pl.when(hor > 0)
    def _():
        base_copy.wait_send()
        for u in range(3):
            rest_copy(u).wait_send()


def write(a, b, a_out, b_out, sem):
    copies = [pltpu.make_async_copy(x, y, sem.at[i]) for i, (x, y) in enumerate([(a, a_out), (b, b_out)])]
    for copy in copies:
        copy.start()
    for copy in copies:
        copy.wait()


def body(
    n_hor,
    n_lat,
    window,
    fresh_noise,
    level_index,
    plan,
    retention,
    lift_weight,
    mod_scale,
    mod_shift,
    conv_weight,
    out_weight,
):
    frames, chans, rows, lon = window.shape
    hidden = conv_weight.shape[1]
    half = hidden // 2
    cpad = -(-chans // 16) * 16
    peers = max(1, n_hor - 1)
    vmem = pl.BlockSpec(memory_space=pltpu.VMEM)
    hbm = pl.BlockSpec(memory_space=pltpu.HBM)
    flat = jax.ShapeDtypeStruct((chans * rows, lon), F32)
    dma = pltpu.SemaphoreType.DMA
    current, arriving = pl.pallas_call(
        functools.partial(kernel, rows, lon, n_hor, n_lat),
        out_shape=(pltpu.VMEM(flat.shape, F32), pltpu.VMEM(flat.shape, F32)),
        in_specs=[hbm] * 10,
        out_specs=(vmem, vmem),
        scratch_shapes=[
            pltpu.SMEM(level_index.shape, jnp.int32),
            pltpu.SMEM(plan.shape, F32),
            pltpu.VMEM((chans * rows, lon), F32),
            pltpu.VMEM((1, hidden), F32),
            pltpu.VMEM((1, hidden), F32),
            pltpu.VMEM((1, hidden), F32),
            pltpu.VMEM((chans, hidden), BF16),
            pltpu.VMEM(conv_weight.shape, BF16),
            pltpu.VMEM((chans, hidden), BF16),
            pltpu.VMEM((hidden, chans), BF16),
            pltpu.VMEM((hidden, 9 * hidden), BF16),
            pltpu.VMEM((rows, cpad, lon), BF16),
            pltpu.VMEM((rows, cpad, lon), BF16),
            pltpu.VMEM((rows, cpad, lon), BF16),
            pltpu.VMEM((rows, cpad, lon), BF16),
            pltpu.VMEM((rows, chans, lon), F32),
            pltpu.VMEM((rows + 2, 3 * hidden, lon), BF16),
            pltpu.VMEM((rows, hidden, lon), F32),
            pltpu.VMEM((rows // POOL, hidden, lon), F32),
            pltpu.VMEM((peers, half, lon), F32),
            pltpu.VMEM((2, hidden, lon), F32),
            pltpu.VMEM((2, hidden, lon), F32),
            pltpu.VMEM((rows * lon, lon), BF16),
            pltpu.VMEM((2, 2 * lon, 2 * lon), BF16),
            pltpu.VMEM((half, lon), F32),
            pltpu.VMEM((STEPS + 1, 2, cpad, lon), BF16),
            pltpu.VMEM((STEPS, 2, cpad, lon), BF16),
            pltpu.VMEM((STEPS, half, lon), WIRE),
            pltpu.VMEM((STEPS, peers, half, lon), WIRE),
            pltpu.VMEM((peers, 1, hidden), F32),
            dma((STEPS, 2)),
            dma((STEPS, 2)),
            dma((STEPS, peers)),
            dma((STEPS, peers)),
            dma((peers,)),
            dma((peers,)),
            dma((10,)),
            dma((8,)),
        ],
        compiler_params=pltpu.CompilerParams(
            collective_id=0, has_side_effects=True, vmem_limit_bytes=66400000
        ),
    )(
        level_index,
        plan,
        window.reshape(chans * rows, lon),
        fresh_noise.reshape(chans * rows, lon),
        retention,
        mod_scale.reshape(1, hidden),
        mod_shift.reshape(1, hidden),
        lift_weight.T,
        conv_weight,
        out_weight,
    )
    shape = (frames, chans, rows, lon)
    current, rolled = pl.pallas_call(
        write,
        out_shape=(flat, flat),
        in_specs=[vmem, vmem],
        out_specs=(hbm, hbm),
        scratch_shapes=[dma((2,))],
        compiler_params=pltpu.CompilerParams(vmem_limit_bytes=4 * 1024 * 1024),
    )(current, arriving)
    return (current.reshape(shape), rolled.reshape(shape))


def solution(mesh):
    in_specs = (
        P("hor", None, "lat", None),
        P(None, "lat", None),
        P("hor"),
        P(),
        P("hor", None),
        P(),
        P(),
        P(),
        P(),
        P(),
    )
    out_specs = (P("hor", None, "lat", None), P("hor", None, "lat", None))
    run = functools.partial(body, mesh.shape["hor"], mesh.shape["lat"])
    return jax.shard_map(run, mesh=mesh, in_specs=in_specs, out_specs=out_specs, check_vma=False)
```

```python
import functools

import jax
import jax.numpy as jnp
from jax import lax
from jax.experimental import pallas as pl
from jax.experimental.pallas import tpu as pltpu
from jax.sharding import PartitionSpec as P

POOL = 4
STEPS = 3
MESH = pl.DeviceIdType.MESH
F32 = jnp.float32
BF16 = jnp.bfloat16
WIRE = jnp.bfloat16


def dot(a, b):
    return jnp.dot(a, b, preferred_element_type=F32)


def kernel(
    rows,
    lon,
    n_hor,
    n_lat,
    lvl_h,
    plan_h,
    win_h,
    fresh_h,
    ret_h,
    msc_h,
    msh_h,
    lift_h,
    convw_h,
    outw_h,
    wout,
    arr,
    lvl,
    plan,
    win,
    rets,
    rfar,
    msc,
    msh,
    liftt,
    convw,
    outw,
    liftw,
    taps,
    home,
    feats0,
    csend,
    xsend,
    xrecv,
    cur,
    stack,
    fsend,
    frecv,
    acc,
    up,
    mods,
    smsh,
    sig,
    poolm,
    spread,
    rate,
    coef,
    far,
    hsend,
    hrecv,
    psend,
    precv,
    qsend,
    qrecv,
    base_send,
    base_recv,
    rest_send,
    rest_recv,
    fin_recv,
    l_sem,
    c_sem,
    g_sem,
    h_sem,
    h0_sem,
    f_sem,
    p_sem,
    q_ssem,
    q_rsem,
    rf_ssem,
    rf_rsem,
    r_ssem,
    r_rsem,
    e_sem,
):
    hidden, chans = liftw.shape
    half = hidden // 2
    n_chip = n_hor // 2
    hor = lax.axis_index("hor")
    lat = lax.axis_index("lat")
    chip = hor // 2
    core = lax.rem(hor, 2)
    other = 1 - core
    outer = core == 1
    partner = {"hor": hor + 1 - 2 * core}
    n_near = jnp.where(lat > 0, 1, 0) + jnp.where(lat < n_lat - 1, 1, 0)

    def has(side):
        return lat > 0 if side == 0 else lat < n_lat - 1

    def remote(src, dst, ssem, rsem, where):
        return pltpu.make_async_remote_copy(
            src_ref=src,
            dst_ref=dst,
            send_sem=ssem,
            recv_sem=rsem,
            device_id=where,
            device_id_type=MESH,
        )

    barrier = pltpu.get_barrier_semaphore()

    def greet(where):
        pl.semaphore_signal(barrier, inc=1, device_id=where, device_id_type=MESH)

    for side in range(2):
        near = lat - 1 + 2 * side

        @pl.when(has(side))
        def _():
            greet({"hor": 2 * chip + 1, "lat": near})

        @pl.when(has(side) & outer)
        def _():
            greet({"hor": 2 * chip, "lat": near})

    for d in range(1, n_hor):
        greet({"hor": lax.rem(hor + d, n_hor)})

    pairs = [(win_h, win), (lvl_h, lvl), (plan_h, plan)]
    pairs += [(msc_h, msc), (msh_h, msh), (ret_h, rets.at[core]), (lift_h, liftt)]
    pairs += [(convw_h, convw), (outw_h, outw)]
    loads = [pltpu.make_async_copy(a, b, l_sem.at[i]) for i, (a, b) in enumerate(pairs)]
    fresh_load = pltpu.make_async_copy(fresh_h, arr, l_sem.at[len(pairs)])
    for load in loads:
        load.start()

    @pl.when(hor == n_hor - 1)
    def _():
        fresh_load.start()

    for side in range(2):

        @pl.when(outer & jnp.logical_not(has(side)))
        def _():
            hrecv[:, side] = jnp.zeros_like(hrecv[:, side])

    for f in range(2):
        for g in range(2):
            for block in (0, 3):
                stack[f, g, block] = jnp.zeros_like(stack[f, g, block])

    def column(row_ref_value, start, count):
        sub = lax.broadcasted_iota(jnp.int32, (count, hidden), 0) + start
        lane = lax.broadcasted_iota(jnp.int32, (count, hidden), 1)
        return jnp.sum(jnp.where(sub == lane, row_ref_value, 0.0), axis=1, keepdims=True)

    def packed_rate(value):
        lane = lax.broadcasted_iota(jnp.int32, (half, lon), 1)
        lo = jnp.broadcast_to(column(value, 0, half), (half, lon))
        hi = jnp.broadcast_to(column(value, half, half), (half, lon))
        return jnp.where(lane < lon // 2, lo, hi)

    groups = lon // POOL
    shift = POOL.bit_length() - 1
    k = lax.broadcasted_iota(jnp.int32, (4 * lon, lon), 0)
    n = lax.broadcasted_iota(jnp.int32, (4 * lon, lon), 1)
    want = lax.shift_right_logical(k, lon.bit_length()) * groups + lax.shift_right_logical(
        lax.bitwise_and(k, lon - 1), shift
    )
    poolm[...] = jnp.where(want == n, 1.0 / (POOL * POOL), 0.0).astype(BF16)
    for side in range(2):
        k = lax.broadcasted_iota(jnp.int32, (2 * lon, 2 * lon), 0)
        n = lax.broadcasted_iota(jnp.int32, (2 * lon, 2 * lon), 1)
        want = side * (lon // 2) + lax.shift_right_logical(n, shift)
        spread[side] = jnp.where(lax.bitwise_and(k, lon - 1) == want, 1.0, 0.0).astype(BF16)

    def in_scale_of(now):
        return 1.0 / jnp.sqrt(now * now + 1.0)

    def outer_row(g, r):
        return g * (rows - 2) + r

    def inner_row(g, r):
        return 2 + 2 * g + r

    def my_row(g, r):
        return jnp.where(outer, outer_row(g, r), inner_row(g, r))

    def their_row(g, r):
        return jnp.where(outer, inner_row(g, r), outer_row(g, r))

    def joint(g):
        return jnp.where(outer, 1 - g, g)

    sig_copy = remote(sig.at[core], sig.at[core], g_sem.at[0], g_sem.at[1], partner)
    ret_copy = remote(rets.at[core], rets.at[core], g_sem.at[2], g_sem.at[3], partner)
    cur_copy = remote(csend, cur.at[core], c_sem.at[0], c_sem.at[1], partner)
    x_copy = remote(xsend, xrecv, c_sem.at[2], c_sem.at[3], partner)

    def first_halo(side, f):
        return remote(
            hsend.at[0, side, f],
            hrecv.at[0, 1 - side, f],
            h0_sem.at[0, side, f],
            h0_sem.at[1, 1 - side, f],
            {"hor": 2 * chip + 1, "lat": lat - 1 + 2 * side},
        )

    def halo_copy(s, side):
        return remote(
            hsend.at[s, side],
            hrecv.at[s, 1 - side],
            h_sem.at[0, s, side],
            h_sem.at[1, s, 1 - side],
            {"lat": lat - 1 + 2 * side},
        )

    def feat_copy(s):
        return remote(fsend.at[s], frecv.at[s], f_sem.at[0, s], f_sem.at[1, s], partner)

    def pool_copy(s):
        return remote(psend.at[s], precv.at[s], p_sem.at[0, s], p_sem.at[1, s], partner)

    def far_pool_copy(s, d, to):
        return remote(
            qsend.at[s],
            qrecv.at[s, d - 1, core],
            q_ssem.at[s, d - 1, to],
            q_rsem.at[s, d - 1, core],
            {"hor": 2 * (chip + d) + to},
        )

    def far_pool_wait(s, d, c):
        return remote(
            qsend.at[s],
            qrecv.at[s, d - 1, c],
            q_ssem.at[s, d - 1, 0],
            q_rsem.at[s, d - 1, c],
            {"hor": 2 * chip + c},
        )

    def far_rate_copy(d, to, c):
        return remote(
            rets.at[core],
            rfar.at[d - 1, c],
            rf_ssem.at[d - 1, to],
            rf_rsem.at[d - 1, c],
            {"hor": 2 * (chip + d) + to},
        )

    back = {"hor": 2 * chip - 1}

    def base_copy(c):
        return remote(base_send, base_recv.at[c], r_ssem.at[0], r_rsem.at[0, c], back)

    def rest_copy(stage, c):
        return remote(
            rest_send.at[stage],
            rest_recv.at[c, stage],
            r_ssem.at[1 + stage],
            r_rsem.at[1 + stage, c],
            back,
        )

    def final_copy(f):
        return remote(cur.at[f], fin_recv.at[f], e_sem.at[0, f], e_sem.at[1, f], partner)

    def half_silu(h):
        return h + h * jnp.tanh(h)

    def shifted(feat):
        ahead = pltpu.roll(feat, 1, 1).astype(BF16)
        behind = pltpu.roll(feat, lon - 1, 1).astype(BF16)
        return jnp.concatenate([ahead, feat.astype(BF16), behind], axis=0)

    low = slice(hidden, 2 * hidden)

    def place(feat, f, g, r):
        parts = shifted(feat)
        stack[f, g, 1 + r] = parts
        if (g, r) == (0, 1):
            stack[f, 1, jnp.where(outer, 4, 0)] = parts
        if (g, r) == (1, 0):
            stack[f, 0, jnp.where(outer, 4, 3)] = parts

    def packed(value):
        return value[0:half] + pltpu.roll(value[half:hidden], lon // 2, 1)

    def set_modulation(s, f):
        log_sigma = jnp.log(sig[f, pl.ds(s, 1), :])
        smsh[f, 0] = 0.5 * (1.0 + log_sigma * mods[0])
        smsh[f, 1] = 0.5 * (log_sigma * mods[1])

    def send_far_pool(s):
        qsend[s] = (rate[1] * psend[s, 0] + psend[s, 1]).astype(WIRE)
        for d in range(1, n_chip):
            for to in range(2):

                @pl.when(chip + d < n_chip)
                def _():
                    far_pool_copy(s, d, to).start()

    for load in loads[0:3]:
        load.wait()
    sub = lax.broadcasted_iota(jnp.int32, (sig.shape[1], lon), 0)
    levels = jnp.ones((sig.shape[1], lon), F32)
    for s in range(STEPS + 1):
        levels = jnp.where(sub == s, plan[jnp.maximum(lvl[0] - s, 0)], levels)
    sig[core] = levels
    scale = in_scale_of(levels[0:1, :])
    for side, row in enumerate((0, rows - 1)):
        edge_row = win[pl.ds(row, chans, stride=rows), :]
        hsend[0, side, core, 0:chans, :] = (edge_row * scale).astype(BF16)
    for row in range(rows):
        home[row] = win[pl.ds(row, chans, stride=rows), :]
    for g in range(2):
        for r in range(2):
            csend[g, r] = home[their_row(g, r)]
            cur[core, g, r] = home[my_row(g, r)]
    for load in loads[3:7]:
        load.wait()
    mods[0] = jnp.broadcast_to(column(msc[...], 0, hidden), (hidden, lon))
    mods[1] = jnp.broadcast_to(column(msh[...], 0, hidden), (hidden, lon))
    eye = (
        lax.broadcasted_iota(jnp.int32, (chans, chans), 0)
        == lax.broadcasted_iota(jnp.int32, (chans, chans), 1)
    ).astype(F32).astype(BF16)
    liftw[...] = lax.dot_general(
        liftt[...], eye, (((0,), (0,)), ((), ())), preferred_element_type=F32
    ).astype(BF16)
    pl.semaphore_wait(barrier, n_hor - 1 + n_near * (1 + core))
    for side in range(2):

        @pl.when(has(side))
        def _():
            first_halo(side, core).start()

    sig_copy.start()
    ret_copy.start()
    cur_copy.start()
    for d in range(1, n_chip - 1):
        for to in range(2):

            @pl.when((chip >= 1) & (chip + d < n_chip))
            def _():
                far_rate_copy(d, to, core).start()

    set_modulation(0, core)
    for p in range(rows // 2):
        scaled = jnp.concatenate(
            [(home[2 * p + i] * scale).astype(BF16) for i in range(2)], axis=1
        )
        lifted = dot(liftw[...], scaled)
        for i in range(2):
            h = lifted[:, i * lon : (i + 1) * lon] * smsh[core, 0] + smsh[core, 1]
            feats0[2 * p + i] = half_silu(h).astype(BF16)
    for g in range(2):
        for r in range(2):
            xsend[2 * g + r] = feats0[their_row(g, r)]
        xsend[4 + g] = feats0[jnp.where(outer, 1 + g * (rows - 3), 2 + g * (rows - 5))]
    x_copy.start()
    pooled = jnp.zeros((hidden, lon), F32)
    for first in (0, 2):
        flat = [feats0[first + 4 * g + r] for g in range(2) for r in range(2)]
        pooled = pooled + dot(jnp.concatenate(flat, axis=1), poolm[...])
    psend[0, core] = packed(pooled)
    psend[0, other] = jnp.zeros((half, lon), F32)
    pool_copy(0).start()
    rate[core] = packed_rate(rets[core])
    for g in range(2):
        for r in range(2):
            place(feats0[my_row(g, r)].astype(F32), core, g, r)
        frecv[0, g, core] = feats0[jnp.where(outer, 2 + g * (rows - 5), 1 + g * (rows - 3))]
    remote(rets.at[other], rets.at[other], g_sem.at[2], g_sem.at[3], partner).wait_recv()
    rate[other] = packed_rate(rets[other])
    send_far_pool(0)
    remote(sig.at[other], sig.at[other], g_sem.at[0], g_sem.at[1], partner).wait_recv()
    set_modulation(0, other)
    for load in loads[7:]:
        load.wait()
    taps[...] = jnp.concatenate([convw[a] for a in range(3)], axis=1)
    x_copy.wait_recv()
    for g in range(2):
        for r in range(2):
            place(xrecv[2 * g + r].astype(F32), other, g, r)
        frecv[0, g, other] = xrecv[4 + g]
    remote(csend, cur.at[other], c_sem.at[0], c_sem.at[1], partner).wait_recv()
    for d in range(1, n_chip - 1):

        @pl.when(chip > d)
        def _():
            for c in range(2):
                far_rate_copy(d, 0, c).wait_recv()
            pair = packed_rate(rfar[d - 1, 0]) * packed_rate(rfar[d - 1, 1])
            coef[d] = pair if d == 1 else coef[d - 1] * pair

    @pl.loop(0, STEPS)
    def _(s):
        final = s == STEPS - 1
        keep, gain, scale_next = [], [], []
        for f in range(2):
            now, after = sig[f, pl.ds(s, 1), :], sig[f, pl.ds(s + 1, 1), :]
            ratio = after / now
            keep.append(ratio + (1.0 - ratio) / (now * now + 1.0))
            gain.append((1.0 - ratio) * (now * in_scale_of(now)))
            scale_next.append(in_scale_of(after))

        @pl.when(final & (chip > 0))
        def _():
            for g in range(2):
                for r in range(2):
                    base_send[g, r, 0:chans, :] = (keep[0] * cur[0, g, r]).astype(BF16)
            base_copy(core).start()

        for f in range(2):
            for g in range(2):
                wide = [
                    jnp.concatenate([stack[f, g, a], stack[f, g, a + 1]], axis=1)
                    for a in range(3)
                ]
                total = dot(taps[...], jnp.concatenate(wide, axis=0))
                for r in range(2):
                    acc[f, g, r] = total[:, r * lon : (r + 1) * lon]

        @pl.when(s > 0)
        def _():
            feat_copy(s).wait_recv()

        for g in range(2):
            rhs = [shifted(frecv[s, g, f].astype(F32)) for f in range(2)]
            extra = dot(convw[2 * joint(g)], jnp.concatenate(rhs, axis=1))
            for f in range(2):
                acc[f, g, joint(g)] += extra[:, f * lon : (f + 1) * lon]

        def remote_edges():
            for side in range(2):

                @pl.when(has(side) & (s == 0))
                def _():
                    for f in range(2):
                        first_halo(1 - side, f).wait_recv()

                @pl.when(has(side) & (s > 0))
                def _():
                    halo_copy(s, 1 - side).wait_recv()

            near = [hrecv[s, side, f, 0:chans, :] for side in range(2) for f in range(2)]
            near = dot(liftw[...], jnp.concatenate(near, axis=1))
            for side in range(2):
                rhs = []
                for f in range(2):
                    at = (2 * side + f) * lon
                    h = near[:, at : at + lon] * smsh[f, 0] + smsh[f, 1]
                    rhs.append(shifted(jnp.where(has(side), half_silu(h), 0.0)))
                extra = dot(convw[2 * side], jnp.concatenate(rhs, axis=1))
                for f in range(2):
                    acc[f, side, side] += extra[:, f * lon : (f + 1) * lon]

        def contexts():
            far[...] = jnp.zeros_like(far)
            for d in range(1, n_chip):

                @pl.when(chip >= d)
                def _():
                    for c in range(2):
                        far_pool_wait(s, d, c).wait_recv()
                    got = qrecv[s, d - 1, 0].astype(F32) + qrecv[s, d - 1, 1].astype(F32)
                    far[...] += got if d == 1 else coef[d - 1] * got

            pool_copy(s).wait_recv()
            first = rate[0] * far[...] + (psend[s, 0] + precv[s, 0])
            second = rate[1] * first + (psend[s, 1] + precv[s, 1])
            both = []
            for total in (first, second):
                high = total.astype(BF16)
                both.append(jnp.concatenate([high, (total - high.astype(F32)).astype(BF16)], axis=1))
            both = jnp.concatenate(both, axis=0)
            for side in range(2):
                wide = dot(both, spread[side])
                for f in range(2):
                    for tok in range(2):
                        up[f, tok, side * half : (side + 1) * half, :] = wide[
                            f * half : (f + 1) * half, tok * lon : (tok + 1) * lon
                        ]

        def finish(stage):
            cells = [(f, g, g if stage else 1 - g) for g in range(2) for f in range(2)]
            gated = []
            for f, g, r in cells:
                feat = stack[f, g, 1 + r, low].astype(F32)
                gated.append(half_silu(0.5 * (feat + acc[f, g, r] + up[f, g])).astype(BF16))
            outputs = dot(outw[...], jnp.concatenate(gated, axis=1))
            for i, (f, g, r) in enumerate(cells):
                nxt = keep[f] * cur[f, g, r] + gain[f] * outputs[:, i * lon : (i + 1) * lon]
                cur[f, g, r] = nxt
                if stage:
                    hsend[s + 1, g, f, 0:chans, :] = (nxt * scale_next[f]).astype(BF16)
                if f == 0:
                    rest_send[stage, g, 0:chans, :] = (
                        nxt - base_send[g, r, 0:chans, :].astype(F32)
                    ).astype(BF16)

            if stage:
                for side in range(2):

                    @pl.when(jnp.logical_not(final) & outer & has(side))
                    def _():
                        halo_copy(s + 1, side).start()

            @pl.when(final & (chip > 0))
            def _():
                rest_copy(stage, core).start()

        contexts()
        finish(0)

        @pl.when(outer)
        def _():
            remote_edges()

        finish(1)

        @pl.when(jnp.logical_not(final))
        def _():
            for f in range(2):
                set_modulation(s + 1, f)
            for f in range(2):
                for g in range(2):
                    scaled = jnp.concatenate(
                        [(cur[f, g, r] * scale_next[f]).astype(BF16) for r in range(2)], axis=1
                    )
                    lifted = dot(liftw[...], scaled)
                    for r in range(2):
                        h = lifted[:, r * lon : (r + 1) * lon] * smsh[f, 0] + smsh[f, 1]
                        place(half_silu(h), f, g, r)
            for g in range(2):
                for f in range(2):
                    fsend[s + 1, g, f] = stack[f, g, 1 + joint(g), low]
            feat_copy(s + 1).start()
            flat = [
                jnp.concatenate([stack[f, g, 1 + r, low] for g in range(2) for r in range(2)], axis=1)
                for f in range(2)
            ]
            pooled = dot(jnp.concatenate(flat, axis=0), poolm[...])
            for f in range(2):
                psend[s + 1, f] = packed(pooled[f * hidden : (f + 1) * hidden])
            pool_copy(s + 1).start()
            send_far_pool(s + 1)

    final_copy(1).start()

    @pl.when(outer)
    def _():
        final_copy(0).start()

    def put(out, row, value):
        out[pl.ds(row, chans, stride=rows), :] = value

    cells = [(g, r) for g in range(2) for r in range(2)]

    @pl.when(outer)
    def _():
        for g, r in cells:
            put(wout, outer_row(g, r), cur[1, g, r])

        final_copy(1).wait_recv()
        for g, r in cells:
            put(wout, inner_row(g, r), fin_recv[1, g, r])

        @pl.when(chip == n_chip - 1)
        def _():
            fresh_load.wait()
            arr[...] = plan[plan.shape[0] - 1] * arr[...]

        @pl.when(chip < n_chip - 1)
        def _():
            for c in range(2):
                base_copy(c).wait_recv()
            for stage in range(2):
                for c in range(2):
                    rest_copy(stage, c).wait_recv()
                    for g in range(2):
                        r = g if stage else 1 - g
                        row = outer_row(g, r) if c else inner_row(g, r)
                        value = base_recv[c, g, r, 0:chans, :].astype(F32)
                        put(arr, row, value + rest_recv[c, stage, g, 0:chans, :].astype(F32))

    @pl.when(jnp.logical_not(outer))
    def _():
        for g, r in cells:
            put(wout, inner_row(g, r), cur[0, g, r])
            put(arr, inner_row(g, r), cur[1, g, r])
        for f, out in ((1, arr), (0, wout)):
            final_copy(f).wait_recv()
            for g, r in cells:
                put(out, outer_row(g, r), fin_recv[f, g, r])

    for copy in (sig_copy, ret_copy, cur_copy, x_copy, final_copy(1)):
        copy.wait_send()
    for side in range(2):

        @pl.when(has(side))
        def _():
            first_halo(side, core).wait_send()

    for d in range(1, n_chip):
        for to in range(2):

            @pl.when(chip + d < n_chip)
            def _():
                for s in range(STEPS):
                    far_pool_copy(s, d, to).wait_send()

    for d in range(1, n_chip - 1):
        for to in range(2):

            @pl.when((chip >= 1) & (chip + d < n_chip))
            def _():
                far_rate_copy(d, to, core).wait_send()

    for s in range(STEPS):
        pool_copy(s).wait_send()
        if s:
            feat_copy(s).wait_send()
            for side in range(2):

                @pl.when(outer & has(side))
                def _():
                    halo_copy(s, side).wait_send()

    @pl.when(outer)
    def _():
        final_copy(0).wait_send()

    @pl.when(chip > 0)
    def _():
        base_copy(core).wait_send()
        for stage in range(2):
            rest_copy(stage, core).wait_send()


def write(a, b, a_out, b_out, sem):
    copies = [pltpu.make_async_copy(x, y, sem.at[i]) for i, (x, y) in enumerate([(a, a_out), (b, b_out)])]
    for copy in copies:
        copy.start()
    for copy in copies:
        copy.wait()


def body(
    n_hor,
    n_lat,
    window,
    fresh_noise,
    level_index,
    plan,
    retention,
    lift_weight,
    mod_scale,
    mod_shift,
    conv_weight,
    out_weight,
):
    frames, chans, rows, lon = window.shape
    hidden = conv_weight.shape[1]
    half = hidden // 2
    cpad = -(-chans // 16) * 16
    n_chip = n_hor // 2
    peers = max(1, n_chip - 1)
    vmem = pl.BlockSpec(memory_space=pltpu.VMEM)
    hbm = pl.BlockSpec(memory_space=pltpu.HBM)
    flat = jax.ShapeDtypeStruct((chans * rows, lon), F32)
    dma = pltpu.SemaphoreType.DMA
    current, arriving = pl.pallas_call(
        functools.partial(kernel, rows, lon, n_hor, n_lat),
        out_shape=(pltpu.VMEM(flat.shape, F32), pltpu.VMEM(flat.shape, F32)),
        in_specs=[hbm] * 10,
        out_specs=(vmem, vmem),
        scratch_shapes=[
            pltpu.SMEM(level_index.shape, jnp.int32),
            pltpu.SMEM(plan.shape, F32),
            pltpu.VMEM((chans * rows, lon), F32),
            pltpu.VMEM((2, 1, hidden), F32),
            pltpu.VMEM((peers, 2, 1, hidden), F32),
            pltpu.VMEM((1, hidden), F32),
            pltpu.VMEM((1, hidden), F32),
            pltpu.VMEM((chans, hidden), BF16),
            pltpu.VMEM(conv_weight.shape, BF16),
            pltpu.VMEM((chans, hidden), BF16),
            pltpu.VMEM((hidden, chans), BF16),
            pltpu.VMEM((hidden, 9 * hidden), BF16),
            pltpu.VMEM((rows, chans, lon), F32),
            pltpu.VMEM((rows, hidden, lon), BF16),
            pltpu.VMEM((2, 2, chans, lon), F32),
            pltpu.VMEM((6, hidden, lon), BF16),
            pltpu.VMEM((6, hidden, lon), BF16),
            pltpu.VMEM((2, 2, 2, chans, lon), F32),
            pltpu.VMEM((2, 2, 5, 3 * hidden, lon), BF16),
            pltpu.VMEM((STEPS, 2, 2, hidden, lon), BF16),
            pltpu.VMEM((STEPS, 2, 2, hidden, lon), BF16),
            pltpu.VMEM((2, 2, 2, hidden, lon), F32),
            pltpu.VMEM((2, 2, hidden, lon), F32),
            pltpu.VMEM((2, hidden, lon), F32),
            pltpu.VMEM((2, 2, hidden, lon), F32),
            pltpu.VMEM((2, 8, lon), F32),
            pltpu.VMEM((4 * lon, lon), BF16),
            pltpu.VMEM((2, 2 * lon, 2 * lon), BF16),
            pltpu.VMEM((2, half, lon), F32),
            pltpu.VMEM((peers, half, lon), F32),
            pltpu.VMEM((half, lon), F32),
            pltpu.VMEM((STEPS + 1, 2, 2, cpad, lon), BF16),
            pltpu.VMEM((STEPS, 2, 2, cpad, lon), BF16),
            pltpu.VMEM((STEPS, 2, half, lon), F32),
            pltpu.VMEM((STEPS, 2, half, lon), F32),
            pltpu.VMEM((STEPS, half, lon), WIRE),
            pltpu.VMEM((STEPS, peers, 2, half, lon), WIRE),
            pltpu.VMEM((2, 2, cpad, lon), BF16),
            pltpu.VMEM((2, 2, 2, cpad, lon), BF16),
            pltpu.VMEM((2, 2, cpad, lon), BF16),
            pltpu.VMEM((2, 2, 2, cpad, lon), BF16),
            pltpu.VMEM((2, 2, 2, chans, lon), F32),
            dma((10,)),
            dma((4,)),
            dma((4,)),
            dma((2, STEPS, 2)),
            dma((2, 2, 2)),
            dma((2, STEPS)),
            dma((2, STEPS)),
            dma((STEPS, peers, 2)),
            dma((STEPS, peers, 2)),
            dma((peers, 2)),
            dma((peers, 2)),
            dma((3,)),
            dma((3, 2)),
            dma((2, 2)),
        ],
        compiler_params=pltpu.CompilerParams(
            collective_id=0, has_side_effects=True, vmem_limit_bytes=66400000
        ),
    )(
        level_index,
        plan,
        window.reshape(chans * rows, lon),
        fresh_noise.reshape(chans * rows, lon),
        retention,
        mod_scale.reshape(1, hidden),
        mod_shift.reshape(1, hidden),
        lift_weight.T,
        conv_weight,
        out_weight,
    )
    shape = (frames, chans, rows, lon)
    current, rolled = pl.pallas_call(
        write,
        out_shape=(flat, flat),
        in_specs=[vmem, vmem],
        out_specs=(hbm, hbm),
        scratch_shapes=[dma((2,))],
        compiler_params=pltpu.CompilerParams(vmem_limit_bytes=4 * 1024 * 1024),
    )(current, arriving)
    return (current.reshape(shape), rolled.reshape(shape))


def solution(mesh):
    in_specs = (
        P("hor", None, "lat", None),
        P(None, "lat", None),
        P("hor"),
        P(),
        P("hor", None),
        P(),
        P(),
        P(),
        P(),
        P(),
    )
    out_specs = (P("hor", None, "lat", None), P("hor", None, "lat", None))
    run = functools.partial(body, mesh.shape["hor"], mesh.shape["lat"])
    return jax.shard_map(run, mesh=mesh, in_specs=in_specs, out_specs=out_specs, check_vma=False)
```

```python
import functools

import jax
import jax.numpy as jnp
from jax import lax
from jax.experimental import pallas as pl
from jax.experimental.pallas import tpu as pltpu
from jax.sharding import PartitionSpec as P

POOL = 4
STEPS = 3
MESH = pl.DeviceIdType.MESH
F32 = jnp.float32
BF16 = jnp.bfloat16
WIRE = jnp.bfloat16


def dot(a, b):
    return jnp.dot(a, b, preferred_element_type=F32)


def kernel(
    rows,
    lon,
    n_hor,
    n_lat,
    lvl_h,
    plan_h,
    win_h,
    fresh_h,
    ret_h,
    msc_h,
    msh_h,
    lift_h,
    convw_h,
    outw_h,
    wout,
    arr,
    lvl,
    plan,
    win,
    rets,
    rfar,
    msc,
    msh,
    liftt,
    convw,
    outw,
    liftw,
    taps,
    home,
    feats0,
    csend,
    xsend,
    xrecv,
    cur,
    stack_a,
    stack_b,
    fsend,
    frecv,
    acc_a,
    acc_b,
    up,
    mods,
    smsh,
    sig,
    poolm,
    spread,
    rate,
    coef,
    raw_rate,
    hsend,
    hrecv,
    psend,
    precv,
    qsend,
    qrecv,
    base_send,
    base_recv,
    rest_send,
    rest_recv,
    fin_recv,
    l_sem,
    c_sem,
    g_sem,
    h_sem,
    f_sem,
    p_sem,
    q_ssem,
    q_rsem,
    rf_ssem,
    rf_rsem,
    r_ssem,
    r_rsem,
    e_sem,
):
    hidden, chans = liftw.shape
    half = hidden // 2
    n_chip = n_hor // 2
    stack, acc = (stack_a, stack_b), (acc_a, acc_b)
    hor = lax.axis_index("hor")
    lat = lax.axis_index("lat")
    chip = hor // 2
    core = lax.rem(hor, 2)
    other = 1 - core
    outer = core == 1
    partner = {"hor": hor + 1 - 2 * core}
    n_near = jnp.where(lat > 0, 1, 0) + jnp.where(lat < n_lat - 1, 1, 0)

    def has(side):
        return lat > 0 if side == 0 else lat < n_lat - 1

    def remote(src, dst, ssem, rsem, where):
        return pltpu.make_async_remote_copy(
            src_ref=src,
            dst_ref=dst,
            send_sem=ssem,
            recv_sem=rsem,
            device_id=where,
            device_id_type=MESH,
        )

    barrier = pltpu.get_barrier_semaphore()

    def greet(where):
        pl.semaphore_signal(barrier, inc=1, device_id=where, device_id_type=MESH)

    for side in range(2):
        near = lat - 1 + 2 * side

        @pl.when(has(side))
        def _():
            greet({"hor": 2 * chip + 1, "lat": near})

        @pl.when(has(side) & outer)
        def _():
            greet({"hor": 2 * chip, "lat": near})

    for d in range(1, n_hor):
        greet({"hor": lax.rem(hor + d, n_hor)})

    pairs = [(win_h, win), (lvl_h, lvl), (plan_h, plan)]
    pairs += [(msc_h, msc), (msh_h, msh), (ret_h, rets.at[core]), (lift_h, liftt)]
    pairs += [(convw_h, convw), (outw_h, outw)]
    loads = [pltpu.make_async_copy(a, b, l_sem.at[i]) for i, (a, b) in enumerate(pairs)]
    fresh_load = pltpu.make_async_copy(fresh_h, arr, l_sem.at[len(pairs)])
    for load in loads:
        load.start()

    @pl.when(hor == n_hor - 1)
    def _():
        fresh_load.start()

    for side in range(2):

        @pl.when(outer & jnp.logical_not(has(side)))
        def _():
            hrecv[:, side] = jnp.zeros_like(hrecv[:, side])

    for f in range(2):
        for block in (0, 5):
            stack[f][block] = jnp.zeros_like(stack[f][block])

    def column(row_ref_value, start, count):
        sub = lax.broadcasted_iota(jnp.int32, (count, hidden), 0) + start
        lane = lax.broadcasted_iota(jnp.int32, (count, hidden), 1)
        return jnp.sum(jnp.where(sub == lane, row_ref_value, 0.0), axis=1, keepdims=True)

    def packed_rate(value):
        lane = lax.broadcasted_iota(jnp.int32, (half, lon), 1)
        lo = jnp.broadcast_to(column(value, 0, half), (half, lon))
        hi = jnp.broadcast_to(column(value, half, half), (half, lon))
        return jnp.where(lane < lon // 2, lo, hi)

    groups = lon // POOL
    shift = POOL.bit_length() - 1
    k = lax.broadcasted_iota(jnp.int32, (4 * lon, lon), 0)
    n = lax.broadcasted_iota(jnp.int32, (4 * lon, lon), 1)
    want = lax.shift_right_logical(k, lon.bit_length()) * groups + lax.shift_right_logical(
        lax.bitwise_and(k, lon - 1), shift
    )
    poolm[...] = jnp.where(want == n, 1.0 / (POOL * POOL), 0.0).astype(BF16)
    for side in range(2):
        k = lax.broadcasted_iota(jnp.int32, (2 * lon, 2 * lon), 0)
        n = lax.broadcasted_iota(jnp.int32, (2 * lon, 2 * lon), 1)
        want = side * (lon // 2) + lax.shift_right_logical(n, shift)
        spread[side] = jnp.where(lax.bitwise_and(k, lon - 1) == want, 1.0, 0.0).astype(BF16)

    def in_scale_of(now):
        return 1.0 / jnp.sqrt(now * now + 1.0)

    def outer_row(g, r):
        return g * (rows - 2) + r

    def inner_row(g, r):
        return 2 + 2 * g + r

    def my_row(g, r):
        return jnp.where(outer, outer_row(g, r), inner_row(g, r))

    def their_row(g, r):
        return jnp.where(outer, inner_row(g, r), outer_row(g, r))

    def joint(g, c):
        return 1 - g if c else g

    sig_copy = remote(sig.at[core], sig.at[core], g_sem.at[0], g_sem.at[1], partner)
    ret_copy = remote(rets.at[core], rets.at[core], g_sem.at[2], g_sem.at[3], partner)
    cur_copy = remote(csend, cur.at[core], c_sem.at[0], c_sem.at[1], partner)
    x_copy = remote(xsend, xrecv, c_sem.at[2], c_sem.at[3], partner)

    def halo_copy(s, side, f):
        return remote(
            hsend.at[s, side, f],
            hrecv.at[s, 1 - side, f],
            h_sem.at[0, s, side, f],
            h_sem.at[1, s, 1 - side, f],
            {"hor": 2 * chip + 1, "lat": lat - 1 + 2 * side},
        )

    def feat_copy(s):
        return remote(fsend.at[s], frecv.at[s], f_sem.at[0, s], f_sem.at[1, s], partner)

    def pool_copy(s):
        return remote(psend.at[s], precv.at[s], p_sem.at[0, s], p_sem.at[1, s], partner)

    def far_pool_copy(s, d, to):
        return remote(
            qsend.at[s],
            qrecv.at[s, d - 1, core],
            q_ssem.at[s, d - 1, to],
            q_rsem.at[s, d - 1, core],
            {"hor": 2 * (chip + d) + to},
        )

    def far_pool_wait(s, d, c):
        return remote(
            qsend.at[s],
            qrecv.at[s, d - 1, c],
            q_ssem.at[s, d - 1, 0],
            q_rsem.at[s, d - 1, c],
            {"hor": 2 * chip + c},
        )

    def far_rate_copy(d, to, c):
        return remote(
            rets.at[core],
            rfar.at[d - 1, c],
            rf_ssem.at[d - 1, to],
            rf_rsem.at[d - 1, c],
            {"hor": 2 * (chip + d) + to},
        )

    back = {"hor": 2 * chip - 1}

    def base_copy(c):
        return remote(base_send, base_recv.at[c], r_ssem.at[0], r_rsem.at[0, c], back)

    def rest_copy(stage, c):
        return remote(
            rest_send.at[stage],
            rest_recv.at[c, stage],
            r_ssem.at[1 + stage],
            r_rsem.at[1 + stage, c],
            back,
        )

    def final_copy(f):
        return remote(cur.at[f], fin_recv.at[f], e_sem.at[0, f], e_sem.at[1, f], partner)

    def half_silu(h):
        return h + h * jnp.tanh(h)

    def shifted(feat):
        ahead = pltpu.roll(feat, 1, 1).astype(BF16)
        behind = pltpu.roll(feat, lon - 1, 1).astype(BF16)
        return jnp.concatenate([ahead, feat.astype(BF16), behind], axis=0)

    low = slice(hidden, 2 * hidden)

    def place(feat, f, g, r):
        stack[f][1 + 2 * g + r] = shifted(feat)

    def feature(f, g, r):
        return stack[f][1 + 2 * g + r, low]

    def convolve(f, c, s):
        for g in range(2):
            blocks = [0, 1, 2, 6 if c else 3] if g == 0 else [7 if c else 2, 3, 4, 5]
            if c:
                stack[f][6 + g] = shifted(frecv[s, g, f].astype(F32))
            wide = [
                jnp.concatenate([stack[f][blocks[a]], stack[f][blocks[a + 1]]], axis=1)
                for a in range(3)
            ]
            total = dot(taps[...], jnp.concatenate(wide, axis=0))
            for r in range(2):
                acc[f][g, r] = total[:, r * lon : (r + 1) * lon]

    def packed(value):
        return value[0:half] + pltpu.roll(value[half:hidden], lon // 2, 1)

    def set_modulation(s, f):
        log_sigma = jnp.log(sig[f, pl.ds(s, 1), :])
        smsh[lax.rem(s, 2), f, 0] = 0.5 * (1.0 + log_sigma * mods[0])
        smsh[lax.rem(s, 2), f, 1] = 0.5 * (log_sigma * mods[1])

    def modulate(value, s, f):
        return half_silu(value * smsh[lax.rem(s, 2), f, 0] + smsh[lax.rem(s, 2), f, 1])

    def send_far_pool(s):
        for d in range(1, n_chip):
            for to in range(2):

                @pl.when(chip + d < n_chip)
                def _():
                    far_pool_copy(s, d, to).start()

    for load in loads[0:3]:
        load.wait()
    sub = lax.broadcasted_iota(jnp.int32, (sig.shape[1], lon), 0)
    levels = jnp.ones((sig.shape[1], lon), F32)
    for s in range(STEPS + 1):
        levels = jnp.where(sub == s, plan[jnp.maximum(lvl[0] - s, 0)], levels)
    sig[core] = levels
    scale = in_scale_of(levels[0:1, :])
    for side, row in enumerate((0, rows - 1)):
        edge_row = win[pl.ds(row, chans, stride=rows), :]
        hsend[0, side, core, 0:chans, :] = (edge_row * scale).astype(BF16)
    for row in range(rows):
        home[row] = win[pl.ds(row, chans, stride=rows), :]
    for g in range(2):
        for r in range(2):
            csend[g, r] = home[their_row(g, r)]
            cur[core, g, r] = home[my_row(g, r)]
            xsend[2 * g + r] = (csend[g, r] * scale).astype(BF16)
        joint_row = jnp.where(outer, 1 + g * (rows - 3), 2 + g * (rows - 5))
        xsend[4 + g] = (home[joint_row] * scale).astype(BF16)
    for load in loads[3:7]:
        load.wait()
    mods[0] = jnp.broadcast_to(column(msc[...], 0, hidden), (hidden, lon))
    mods[1] = jnp.broadcast_to(column(msh[...], 0, hidden), (hidden, lon))
    eye = (
        lax.broadcasted_iota(jnp.int32, (chans, chans), 0)
        == lax.broadcasted_iota(jnp.int32, (chans, chans), 1)
    ).astype(F32).astype(BF16)
    liftw[...] = lax.dot_general(
        liftt[...], eye, (((0,), (0,)), ((), ())), preferred_element_type=F32
    ).astype(BF16)
    set_modulation(0, core)
    for p in range(rows // 2):
        scaled = jnp.concatenate(
            [(home[2 * p + i] * scale).astype(BF16) for i in range(2)], axis=1
        )
        lifted = dot(liftw[...], scaled)
        for i in range(2):
            feats0[2 * p + i] = modulate(lifted[:, i * lon : (i + 1) * lon], 0, core).astype(BF16)
    pl.semaphore_wait(barrier, n_hor - 1 + n_near * (1 + core))
    even = lax.rem(lat, 2) == 0
    send_order = [(0, even), (1, lat >= 0), (0, jnp.logical_not(even))]
    for side, when in send_order:

        @pl.when(has(side) & when)
        def _():
            halo_copy(0, side, core).start()

    sig_copy.start()
    x_copy.start()
    ret_copy.start()
    cur_copy.start()
    pooled = jnp.zeros((hidden, lon), F32)
    for first in (0, 2):
        flat = [feats0[first + 4 * g + r] for g in range(2) for r in range(2)]
        pooled = pooled + dot(jnp.concatenate(flat, axis=1), poolm[...])
    pooled = packed(pooled)
    qsend[0] = pooled.astype(WIRE)
    psend[0, core] = pooled
    psend[0, other] = jnp.zeros((half, lon), F32)
    send_far_pool(0)
    pool_copy(0).start()
    rate[core] = packed_rate(rets[core])
    for d in range(1, n_chip):
        for to in range(2):

            @pl.when(chip + d < n_chip)
            def _():
                far_rate_copy(d, to, core).start()

    for load in loads[7:]:
        load.wait()
    taps[...] = jnp.concatenate([convw[a] for a in range(3)], axis=1)

    for c in range(2):

        @pl.when(core == c)
        def _():
            row_of = outer_row if c else inner_row
            for g in range(2):
                for r in range(2):
                    place(feats0[row_of(g, r)].astype(F32), c, g, r)
                frecv[0, g, c] = feats0[(2 + g * (rows - 5)) if c else (1 + g * (rows - 3))]
            convolve(c, c, 0)
            remote(sig.at[1 - c], sig.at[1 - c], g_sem.at[0], g_sem.at[1], partner).wait_recv()
            set_modulation(0, 1 - c)
            x_copy.wait_recv()
            for p in range(3):
                got = jnp.concatenate([xrecv[2 * p], xrecv[2 * p + 1]], axis=1)
                lifted = dot(liftw[...], got)
                for i in range(2):
                    feat = modulate(lifted[:, i * lon : (i + 1) * lon], 0, 1 - c)
                    if p < 2:
                        place(feat, 1 - c, p, i)
                    else:
                        frecv[0, i, 1 - c] = feat.astype(BF16)
            convolve(1 - c, c, 0)

    remote(rets.at[other], rets.at[other], g_sem.at[2], g_sem.at[3], partner).wait_recv()
    rate[other] = packed_rate(rets[other])
    remote(csend, cur.at[other], c_sem.at[0], c_sem.at[1], partner).wait_recv()
    def far_rates():
        for d in range(1, n_chip):

            @pl.when(chip >= d)
            def _():
                for c in range(2):
                    far_rate_copy(d, 0, c).wait_recv()
                second = packed_rate(rfar[d - 1, 1])
                raw_rate[d - 1] = second
                if d < n_chip - 1:
                    pair = packed_rate(rfar[d - 1, 0]) * second
                    coef[d] = pair if d == 1 else coef[d - 1] * pair

    def step(s, final):
        keep, gain, scale_next = [], [], []
        for f in range(2):
            now, after = sig[f, pl.ds(s, 1), :], sig[f, pl.ds(s + 1, 1), :]
            ratio = after / now
            keep.append(ratio + (1.0 - ratio) / (now * now + 1.0))
            gain.append((1.0 - ratio) * (now * in_scale_of(now)))
            scale_next.append(in_scale_of(after))

        if not final:

            @pl.when((s == STEPS - 2) & (chip > 0))
            def _():
                last, end = sig[0, pl.ds(s + 1, 1), :], sig[0, pl.ds(s + 2, 1), :]
                hold = keep[0] * (end / last + (1.0 - end / last) / (last * last + 1.0))
                for g in range(2):
                    for r in range(2):
                        base_send[g, r, 0:chans, :] = (hold * cur[0, g, r]).astype(BF16)
                base_copy(core).start()

        def await_feats():
            @pl.when(s > 0)
            def _():
                feat_copy(s).wait_recv()

        def joint_edges(c):
            for g in range(2):
                j = joint(g, c)
                rhs = [shifted(frecv[s, g, f].astype(F32)) for f in range(2)]
                extra = dot(convw[2 * j], jnp.concatenate(rhs, axis=1))
                for f in range(2):
                    acc[f][g, j] += extra[:, f * lon : (f + 1) * lon]

        def await_halos(f):
            for side in range(2):

                @pl.when(has(side))
                def _():
                    halo_copy(s, 1 - side, f).wait_recv()

        def remote_edges(frames):
            near = [hrecv[s, side, f, 0:chans, :] for side in range(2) for f in frames]
            near = dot(liftw[...], jnp.concatenate(near, axis=1))
            for side in range(2):
                rhs = []
                for i, f in enumerate(frames):
                    at = (side * len(frames) + i) * lon
                    feat = modulate(near[:, at : at + lon], s, f)
                    rhs.append(shifted(jnp.where(has(side), feat, 0.0)))
                extra = dot(convw[2 * side], jnp.concatenate(rhs, axis=1))
                for i, f in enumerate(frames):
                    acc[f][side, side] += extra[:, i * lon : (i + 1) * lon]

        def await_pools():
            if not final:

                @pl.when(s == 0)
                def _():
                    far_rates()

            pool_copy(s).wait_recv()
            for d in range(1, n_chip):
                for c in range(2):

                    @pl.when(chip >= d)
                    def _():
                        far_pool_wait(s, d, c).wait_recv()

        def contexts():
            first = psend[s, 0] + precv[s, 0]
            if n_chip > 1:
                total = jnp.zeros((half, lon), F32)
                for d in range(1, n_chip):
                    got = qrecv[s, d - 1, 0].astype(F32)
                    if not final:
                        got = got * jnp.where(s == 0, raw_rate[d - 1], 1.0)
                    got = got + qrecv[s, d - 1, 1].astype(F32)
                    got = got if d == 1 else coef[d - 1] * got
                    total = total + jnp.where(chip >= d, got, 0.0)
                first = first + rate[0] * total
            second = rate[1] * first + (psend[s, 1] + precv[s, 1])
            both = []
            for total in (first, second):
                high = total.astype(BF16)
                both.append(jnp.concatenate([high, (total - high.astype(F32)).astype(BF16)], axis=1))
            both = jnp.concatenate(both, axis=0)
            for side in range(2):
                wide = dot(both, spread[side])
                for f in range(2):
                    for tok in range(2):
                        up[f, tok, side * half : (side + 1) * half, :] = wide[
                            f * half : (f + 1) * half, tok * lon : (tok + 1) * lon
                        ]

        def finish(cells):
            gated = []
            for f, g, r in cells:
                feat = feature(f, g, r).astype(F32)
                gated.append(half_silu(0.5 * (feat + acc[f][g, r] + up[f, g])).astype(BF16))
            outputs = dot(outw[...], jnp.concatenate(gated, axis=1))
            for i, (f, g, r) in enumerate(cells):
                nxt = keep[f] * cur[f, g, r] + gain[f] * outputs[:, i * lon : (i + 1) * lon]
                cur[f, g, r] = nxt
                if g == r and not final:
                    hsend[s + 1, g, f, 0:chans, :] = (nxt * scale_next[f]).astype(BF16)
                if f == 0 and final:
                    rest_send[1 if g == r else 0, g, 0:chans, :] = (
                        nxt - base_send[g, r, 0:chans, :].astype(F32)
                    ).astype(BF16)

        def send_rest(stage):
            @pl.when(chip > 0)
            def _():
                rest_copy(stage, core).start()

        def lift(pairs):
            for pair in pairs:
                f = pair[0][0]
                scaled = jnp.concatenate(
                    [(cur[cell] * scale_next[f]).astype(BF16) for cell in pair], axis=1
                )
                lifted = dot(liftw[...], scaled)
                for i, cell in enumerate(pair):
                    place(modulate(lifted[:, i * lon : (i + 1) * lon], s + 1, f), *cell)

        def send_feats(c):
            for f in range(2):
                for g in range(2):
                    fsend[s + 1, g, f] = feature(f, g, joint(g, c))
            feat_copy(s + 1).start()

        def send_pools():
            flat = [
                jnp.concatenate([feature(f, g, r) for g in range(2) for r in range(2)], axis=1)
                for f in range(2)
            ]
            pooled = dot(jnp.concatenate(flat, axis=0), poolm[...])
            first, second = (packed(pooled[f * hidden : (f + 1) * hidden]) for f in range(2))
            qsend[s + 1] = (rate[1] * first + second).astype(WIRE)
            send_far_pool(s + 1)
            psend[s + 1, 0] = first
            psend[s + 1, 1] = second
            pool_copy(s + 1).start()

        near_cells = [[(f, 0, 1), (f, 1, 0)] for f in range(2)]
        edge_cells = [[(f, 0, 0), (f, 1, 1)] for f in range(2)]

        def send_edges():
            for side, when in send_order:

                @pl.when(has(side) & when)
                def _():
                    for f in range(2):
                        halo_copy(s + 1, side, f).start()

        all_near, all_edge = near_cells[0] + near_cells[1], edge_cells[0] + edge_cells[1]

        @pl.when(outer)
        def _():
            await_pools()
            contexts()
            finish(all_near)
            if final:
                send_rest(0)
            for f in range(2):
                await_halos(f)
            remote_edges([0, 1])
            finish(all_edge)
            if final:
                send_rest(1)
            else:
                send_edges()

            if final:
                for f in range(2):
                    final_copy(f).start()
            else:
                for f in range(2):
                    set_modulation(s + 1, f)
                lift(near_cells)
                send_feats(1)
                lift(edge_cells)
                send_pools()
                feat_copy(s + 1).wait_recv()
                for f in range(2):
                    convolve(f, 1, s + 1)

        @pl.when(jnp.logical_not(outer))
        def _():
            await_feats()
            joint_edges(0)
            await_pools()
            contexts()
            if final:
                finish(near_cells[0] + edge_cells[0])
                send_rest(0)
                send_rest(1)
                finish(near_cells[1] + edge_cells[1])
                final_copy(1).start()
            else:
                finish(near_cells[0] + edge_cells[0])
                finish(near_cells[1] + edge_cells[1])
                for f in range(2):
                    set_modulation(s + 1, f)
                lift(edge_cells)
                send_feats(0)
                lift(near_cells)
                send_pools()
                for f in range(2):
                    convolve(f, 0, s + 1)

    @pl.loop(0, STEPS - 1)
    def _(s):
        step(s, False)

    step(STEPS - 1, True)

    def put(out, row, value):
        out[pl.ds(row, chans, stride=rows), :] = value

    cells = [(g, r) for g in range(2) for r in range(2)]

    @pl.when(outer)
    def _():
        for g, r in cells:
            put(wout, outer_row(g, r), cur[1, g, r])

        final_copy(1).wait_recv()
        for g, r in cells:
            put(wout, inner_row(g, r), fin_recv[1, g, r])

        @pl.when(chip == n_chip - 1)
        def _():
            fresh_load.wait()
            arr[...] = plan[plan.shape[0] - 1] * arr[...]

        @pl.when(chip < n_chip - 1)
        def _():
            for c in range(2):
                base_copy(c).wait_recv()
            for stage in range(2):
                for c in range(2):
                    rest_copy(stage, c).wait_recv()
                    for g in range(2):
                        r = g if stage else 1 - g
                        row = outer_row(g, r) if c else inner_row(g, r)
                        value = base_recv[c, g, r, 0:chans, :].astype(F32)
                        put(arr, row, value + rest_recv[c, stage, g, 0:chans, :].astype(F32))

    @pl.when(jnp.logical_not(outer))
    def _():
        for g, r in cells:
            put(wout, inner_row(g, r), cur[0, g, r])
            put(arr, inner_row(g, r), cur[1, g, r])
        for f, out in ((1, arr), (0, wout)):
            final_copy(f).wait_recv()
            for g, r in cells:
                put(out, outer_row(g, r), fin_recv[f, g, r])

    for copy in (sig_copy, ret_copy, cur_copy, x_copy, final_copy(1)):
        copy.wait_send()
    for side in range(2):

        @pl.when(has(side))
        def _():
            halo_copy(0, side, core).wait_send()

    for d in range(1, n_chip):
        for to in range(2):

            @pl.when(chip + d < n_chip)
            def _():
                for s in range(STEPS):
                    far_pool_copy(s, d, to).wait_send()

    for d in range(1, n_chip):
        for to in range(2):

            @pl.when(chip + d < n_chip)
            def _():
                far_rate_copy(d, to, core).wait_send()

    for s in range(STEPS):
        pool_copy(s).wait_send()
        if s:
            feat_copy(s).wait_send()
            for side in range(2):

                @pl.when(outer & has(side))
                def _():
                    for f in range(2):
                        halo_copy(s, side, f).wait_send()

    @pl.when(outer)
    def _():
        final_copy(0).wait_send()

    @pl.when(chip > 0)
    def _():
        base_copy(core).wait_send()
        for stage in range(2):
            rest_copy(stage, core).wait_send()


def write(a, b, a_out, b_out, sem):
    copies = [pltpu.make_async_copy(x, y, sem.at[i]) for i, (x, y) in enumerate([(a, a_out), (b, b_out)])]
    for copy in copies:
        copy.start()
    for copy in copies:
        copy.wait()


def body(
    n_hor,
    n_lat,
    window,
    fresh_noise,
    level_index,
    plan,
    retention,
    lift_weight,
    mod_scale,
    mod_shift,
    conv_weight,
    out_weight,
):
    frames, chans, rows, lon = window.shape
    hidden = conv_weight.shape[1]
    half = hidden // 2
    cpad = -(-chans // 8) * 8
    n_chip = n_hor // 2
    peers = max(1, n_chip - 1)
    vmem = pl.BlockSpec(memory_space=pltpu.VMEM)
    hbm = pl.BlockSpec(memory_space=pltpu.HBM)
    flat = jax.ShapeDtypeStruct((chans * rows, lon), F32)
    dma = pltpu.SemaphoreType.DMA
    current, arriving = pl.pallas_call(
        functools.partial(kernel, rows, lon, n_hor, n_lat),
        out_shape=(pltpu.VMEM(flat.shape, F32), pltpu.VMEM(flat.shape, F32)),
        in_specs=[hbm] * 10,
        out_specs=(vmem, vmem),
        scratch_shapes=[
            pltpu.SMEM(level_index.shape, jnp.int32),
            pltpu.SMEM(plan.shape, F32),
            pltpu.VMEM((chans * rows, lon), F32),
            pltpu.VMEM((2, 1, hidden), F32),
            pltpu.VMEM((peers, 2, 1, hidden), F32),
            pltpu.VMEM((1, hidden), F32),
            pltpu.VMEM((1, hidden), F32),
            pltpu.VMEM((chans, hidden), BF16),
            pltpu.VMEM(conv_weight.shape, BF16),
            pltpu.VMEM((chans, hidden), BF16),
            pltpu.VMEM((hidden, chans), BF16),
            pltpu.VMEM((hidden, 9 * hidden), BF16),
            pltpu.VMEM((rows, chans, lon), F32),
            pltpu.VMEM((rows, hidden, lon), BF16),
            pltpu.VMEM((2, 2, chans, lon), F32),
            pltpu.VMEM((6, chans, lon), BF16),
            pltpu.VMEM((6, chans, lon), BF16),
            pltpu.VMEM((2, 2, 2, chans, lon), F32),
            pltpu.VMEM((8, 3 * hidden, lon), BF16),
            pltpu.VMEM((8, 3 * hidden, lon), BF16),
            pltpu.VMEM((STEPS, 2, 2, hidden, lon), BF16),
            pltpu.VMEM((STEPS, 2, 2, hidden, lon), BF16),
            pltpu.VMEM((2, 2, hidden, lon), F32),
            pltpu.VMEM((2, 2, hidden, lon), F32),
            pltpu.VMEM((2, 2, hidden, lon), F32),
            pltpu.VMEM((2, hidden, lon), F32),
            pltpu.VMEM((2, 2, 2, hidden, lon), F32),
            pltpu.VMEM((2, 8, lon), F32),
            pltpu.VMEM((4 * lon, lon), BF16),
            pltpu.VMEM((2, 2 * lon, 2 * lon), BF16),
            pltpu.VMEM((2, half, lon), F32),
            pltpu.VMEM((peers, half, lon), F32),
            pltpu.VMEM((peers, half, lon), F32),
            pltpu.VMEM((STEPS + 1, 2, 2, cpad, lon), BF16),
            pltpu.VMEM((STEPS, 2, 2, cpad, lon), BF16),
            pltpu.VMEM((STEPS, 2, half, lon), F32),
            pltpu.VMEM((STEPS, 2, half, lon), F32),
            pltpu.VMEM((STEPS, half, lon), WIRE),
            pltpu.VMEM((STEPS, peers, 2, half, lon), WIRE),
            pltpu.VMEM((2, 2, cpad, lon), BF16),
            pltpu.VMEM((2, 2, 2, cpad, lon), BF16),
            pltpu.VMEM((2, 2, cpad, lon), BF16),
            pltpu.VMEM((2, 2, 2, cpad, lon), BF16),
            pltpu.VMEM((2, 2, 2, chans, lon), F32),
            dma((10,)),
            dma((4,)),
            dma((4,)),
            dma((2, STEPS, 2, 2)),
            dma((2, STEPS)),
            dma((2, STEPS)),
            dma((STEPS, peers, 2)),
            dma((STEPS, peers, 2)),
            dma((peers, 2)),
            dma((peers, 2)),
            dma((3,)),
            dma((3, 2)),
            dma((2, 2)),
        ],
        compiler_params=pltpu.CompilerParams(
            collective_id=0, has_side_effects=True, vmem_limit_bytes=66400000
        ),
    )(
        level_index,
        plan,
        window.reshape(chans * rows, lon),
        fresh_noise.reshape(chans * rows, lon),
        retention,
        mod_scale.reshape(1, hidden),
        mod_shift.reshape(1, hidden),
        lift_weight.T,
        conv_weight,
        out_weight,
    )
    shape = (frames, chans, rows, lon)
    current, rolled = pl.pallas_call(
        write,
        out_shape=(flat, flat),
        in_specs=[vmem, vmem],
        out_specs=(hbm, hbm),
        scratch_shapes=[dma((2,))],
        compiler_params=pltpu.CompilerParams(vmem_limit_bytes=4 * 1024 * 1024),
    )(current, arriving)
    return (current.reshape(shape), rolled.reshape(shape))


def solution(mesh):
    in_specs = (
        P("hor", None, "lat", None),
        P(None, "lat", None),
        P("hor"),
        P(),
        P("hor", None),
        P(),
        P(),
        P(),
        P(),
        P(),
    )
    out_specs = (P("hor", None, "lat", None), P("hor", None, "lat", None))
    run = functools.partial(body, mesh.shape["hor"], mesh.shape["lat"])
    return jax.shard_map(run, mesh=mesh, in_specs=in_specs, out_specs=out_specs, check_vma=False)
```

```python
import functools

import jax
import jax.numpy as jnp
from jax import lax
from jax.experimental import pallas as pl
from jax.experimental.pallas import tpu as pltpu
from jax.sharding import PartitionSpec as P

POOL = 4
STEPS = 3
MESH = pl.DeviceIdType.MESH
F32 = jnp.float32
BF16 = jnp.bfloat16
WIRE = jnp.bfloat16


def dot(a, b):
    return jnp.dot(a, b, preferred_element_type=F32)


def kernel(
    rows,
    lon,
    n_hor,
    n_lat,
    lvl_h,
    plan_h,
    win_h,
    fresh_h,
    ret_h,
    msc_h,
    msh_h,
    lift_h,
    convw_h,
    outw_h,
    wout,
    arr,
    lvl,
    plan,
    win,
    rets,
    rfar,
    msc,
    msh,
    liftt,
    convw,
    outw,
    liftw,
    taps,
    home,
    feats0,
    csend,
    xsend,
    xrecv,
    cur,
    stack_a,
    stack_b,
    fsend,
    frecv,
    acc_a,
    acc_b,
    up,
    mods,
    smsh,
    sig,
    poolm,
    spread,
    rate,
    coef,
    raw_rate,
    hsend,
    hrecv,
    psend,
    precv,
    qsend,
    qrecv,
    base_send,
    base_recv,
    rest_send,
    rest_recv,
    fin_recv,
    l_sem,
    g_sem,
    h_sem,
    f_sem,
    p_sem,
    q_ssem,
    q_rsem,
    rf_ssem,
    rf_rsem,
    r_sem,
    e_sem,
):
    hidden, chans = liftw.shape
    half = hidden // 2
    n_chip = n_hor // 2
    stack, acc = (stack_a, stack_b), (acc_a, acc_b)
    hor = lax.axis_index("hor")
    lat = lax.axis_index("lat")
    chip = hor // 2
    core = lax.rem(hor, 2)
    other = 1 - core
    outer = core == 1
    partner = {"hor": hor + 1 - 2 * core}
    n_near = jnp.where(lat > 0, 1, 0) + jnp.where(lat < n_lat - 1, 1, 0)

    def has(side):
        return lat > 0 if side == 0 else lat < n_lat - 1

    def remote(src, dst, ssem, rsem, where):
        return pltpu.make_async_remote_copy(
            src_ref=src,
            dst_ref=dst,
            send_sem=ssem,
            recv_sem=rsem,
            device_id=where,
            device_id_type=MESH,
        )

    barrier = pltpu.get_barrier_semaphore()

    def greet(where):
        pl.semaphore_signal(barrier, inc=1, device_id=where, device_id_type=MESH)

    for side in range(2):
        near = lat - 1 + 2 * side

        @pl.when(has(side))
        def _():
            greet({"hor": 2 * chip + 1, "lat": near})

        @pl.when(has(side) & outer)
        def _():
            greet({"hor": 2 * chip, "lat": near})

    for d in range(1, n_hor):
        greet({"hor": lax.rem(hor + d, n_hor)})

    pairs = [(lift_h, liftt), (lvl_h, lvl), (plan_h, plan)]
    pairs += [(msc_h, msc), (msh_h, msh), (ret_h, rets.at[core]), (win_h, win)]
    pairs += [(convw_h, convw), (outw_h, outw)]
    loads = [pltpu.make_async_copy(a, b, l_sem.at[i]) for i, (a, b) in enumerate(pairs)]
    fresh_load = pltpu.make_async_copy(fresh_h, arr, l_sem.at[len(pairs)])
    for load in loads:
        load.start()

    @pl.when(hor == n_hor - 1)
    def _():
        fresh_load.start()

    for side in range(2):

        @pl.when(outer & jnp.logical_not(has(side)))
        def _():
            hrecv[:, side] = jnp.zeros_like(hrecv[:, side])

    for f in range(2):
        for block in (0, 5):
            stack[f][block] = jnp.zeros_like(stack[f][block])

    def column(row_ref_value, start, count):
        sub = lax.broadcasted_iota(jnp.int32, (count, hidden), 0) + start
        lane = lax.broadcasted_iota(jnp.int32, (count, hidden), 1)
        return jnp.sum(jnp.where(sub == lane, row_ref_value, 0.0), axis=1, keepdims=True)

    def packed_rate(value):
        lane = lax.broadcasted_iota(jnp.int32, (half, lon), 1)
        lo = jnp.broadcast_to(column(value, 0, half), (half, lon))
        hi = jnp.broadcast_to(column(value, half, half), (half, lon))
        return jnp.where(lane < lon // 2, lo, hi)

    groups = lon // POOL
    shift = POOL.bit_length() - 1
    k = lax.broadcasted_iota(jnp.int32, (4 * lon, lon), 0)
    n = lax.broadcasted_iota(jnp.int32, (4 * lon, lon), 1)
    want = lax.shift_right_logical(k, lon.bit_length()) * groups + lax.shift_right_logical(
        lax.bitwise_and(k, lon - 1), shift
    )
    poolm[...] = jnp.where(want == n, 1.0 / (POOL * POOL), 0.0).astype(BF16)
    for side in range(2):
        k = lax.broadcasted_iota(jnp.int32, (2 * lon, 2 * lon), 0)
        n = lax.broadcasted_iota(jnp.int32, (2 * lon, 2 * lon), 1)
        want = side * (lon // 2) + lax.shift_right_logical(n, shift)
        spread[side] = jnp.where(lax.bitwise_and(k, lon - 1) == want, 1.0, 0.0).astype(BF16)

    def in_scale_of(now):
        return 1.0 / jnp.sqrt(now * now + 1.0)

    def outer_row(g, r):
        return g * (rows - 2) + r

    def inner_row(g, r):
        return 2 + 2 * g + r

    def my_row(g, r):
        return jnp.where(outer, outer_row(g, r), inner_row(g, r))

    def their_row(g, r):
        return jnp.where(outer, inner_row(g, r), outer_row(g, r))

    def joint(g, c):
        return 1 - g if c else g

    sig_copy = remote(sig.at[core], sig.at[core], l_sem.at[2], g_sem.at[0], partner)
    ret_copy = remote(rets.at[core], rets.at[core], l_sem.at[3], g_sem.at[1], partner)
    cur_copy = remote(csend, cur.at[core], l_sem.at[4], g_sem.at[2], partner)
    x_copy = remote(xsend, xrecv, l_sem.at[5], g_sem.at[3], partner)

    def beside(side):
        return {"hor": 2 * chip + 1, "lat": lat - 1 + 2 * side}

    def first_halo(side, f):
        return remote(
            hsend.at[0, side, f],
            hrecv.at[0, 1 - side, f],
            l_sem.at[side],
            h_sem.at[f, 1 - side],
            beside(side),
        )

    def halo_copy(s, side):
        return remote(
            hsend.at[s, side],
            hrecv.at[s, 1 - side],
            l_sem.at[side],
            h_sem.at[2 * lax.rem(s, 2), 1 - side],
            beside(side),
        )

    def feat_copy(s):
        return remote(fsend.at[s], frecv.at[s], l_sem.at[6], f_sem.at[lax.rem(s, 2)], partner)

    def pool_copy(s):
        return remote(psend.at[s], precv.at[s], p_sem.at[2], p_sem.at[lax.rem(s, 2)], partner)

    def far_pool_copy(s, d, to):
        return remote(
            qsend.at[s],
            qrecv.at[s, d - 1, core],
            q_ssem.at[d - 1, to],
            q_rsem.at[s, d - 1, core],
            {"hor": 2 * (chip + d) + to},
        )

    def far_pool_wait(s, d, c):
        return remote(
            qsend.at[s],
            qrecv.at[s, d - 1, c],
            q_ssem.at[d - 1, 0],
            q_rsem.at[s, d - 1, c],
            {"hor": 2 * chip + c},
        )

    def far_rate_copy(d, to, c):
        return remote(
            rets.at[core],
            rfar.at[d - 1, c],
            rf_ssem.at[d - 1, to],
            rf_rsem.at[d - 1, c],
            {"hor": 2 * (chip + d) + to},
        )

    back = {"hor": 2 * chip - 1}

    def base_copy(c):
        return remote(base_send, base_recv.at[c], l_sem.at[2], r_sem.at[c], back)

    def outer_rest(stage):
        return remote(
            rest_send.at[stage],
            rest_recv.at[1, stage],
            l_sem.at[3 + stage],
            r_sem.at[2 + stage],
            back,
        )

    inner_rest = remote(rest_send, rest_recv.at[0], l_sem.at[3], r_sem.at[4], back)

    def final_copy(f):
        return remote(cur.at[f], fin_recv.at[f], l_sem.at[5 + f], e_sem.at[f], partner)

    def half_silu(h):
        return h + h * jnp.tanh(h)

    def shifted(feat):
        ahead = pltpu.roll(feat, 1, 1).astype(BF16)
        behind = pltpu.roll(feat, lon - 1, 1).astype(BF16)
        return jnp.concatenate([ahead, feat.astype(BF16), behind], axis=0)

    low = slice(hidden, 2 * hidden)

    def place(feat, f, g, r):
        stack[f][1 + 2 * g + r] = shifted(feat)

    def feature(f, g, r):
        return stack[f][1 + 2 * g + r, low]

    def convolve(f, c, s):
        for g in range(2):
            blocks = [0, 1, 2, 6 if c else 3] if g == 0 else [7 if c else 2, 3, 4, 5]
            if c:
                stack[f][6 + g] = shifted(frecv[s, g, f].astype(F32))
            wide = [
                jnp.concatenate([stack[f][blocks[a]], stack[f][blocks[a + 1]]], axis=1)
                for a in range(3)
            ]
            total = dot(taps[...], jnp.concatenate(wide, axis=0))
            for r in range(2):
                acc[f][g, r] = total[:, r * lon : (r + 1) * lon]

    def packed(value):
        return value[0:half] + pltpu.roll(value[half:hidden], lon // 2, 1)

    def set_modulation(s, f):
        log_sigma = jnp.log(sig[f, pl.ds(s, 1), :])
        smsh[lax.rem(s, 2), f, 0] = 0.5 * (1.0 + log_sigma * mods[0])
        smsh[lax.rem(s, 2), f, 1] = 0.5 * (log_sigma * mods[1])

    def modulate(value, s, f):
        return half_silu(value * smsh[lax.rem(s, 2), f, 0] + smsh[lax.rem(s, 2), f, 1])

    def send_far_pool(s):
        for d in range(1, n_chip):
            for to in range(2):

                @pl.when(chip + d < n_chip)
                def _():
                    far_pool_copy(s, d, to).start()

    def drain_far_pool(s):
        for d in range(1, n_chip):
            for to in range(2):

                @pl.when(chip + d < n_chip)
                def _():
                    far_pool_copy(s, d, to).wait_send()

    for load in loads[0:6]:
        load.wait()
    sub = lax.broadcasted_iota(jnp.int32, (sig.shape[1], lon), 0)
    levels = jnp.ones((sig.shape[1], lon), F32)
    for s in range(STEPS + 1):
        levels = jnp.where(sub == s, plan[jnp.maximum(lvl[0] - s, 0)], levels)
    sig[core] = levels
    scale = in_scale_of(levels[0:1, :])
    mods[0] = jnp.broadcast_to(column(msc[...], 0, hidden), (hidden, lon))
    mods[1] = jnp.broadcast_to(column(msh[...], 0, hidden), (hidden, lon))
    eye = (
        lax.broadcasted_iota(jnp.int32, (chans, chans), 0)
        == lax.broadcasted_iota(jnp.int32, (chans, chans), 1)
    ).astype(F32).astype(BF16)
    liftw[...] = lax.dot_general(
        liftt[...], eye, (((0,), (0,)), ((), ())), preferred_element_type=F32
    ).astype(BF16)
    set_modulation(0, core)
    loads[6].wait()
    for side, row in enumerate((0, rows - 1)):
        edge_row = win[pl.ds(row, chans, stride=rows), :]
        hsend[0, side, core, 0:chans, :] = (edge_row * scale).astype(BF16)
    for row in range(rows):
        home[row] = win[pl.ds(row, chans, stride=rows), :]
    for g in range(2):
        for r in range(2):
            csend[g, r] = home[their_row(g, r)]
            cur[core, g, r] = home[my_row(g, r)]
            xsend[2 * g + r] = (csend[g, r] * scale).astype(BF16)
        joint_row = jnp.where(outer, 1 + g * (rows - 3), 2 + g * (rows - 5))
        xsend[4 + g] = (home[joint_row] * scale).astype(BF16)
    for p in range(rows // 2):
        scaled = jnp.concatenate(
            [(home[2 * p + i] * scale).astype(BF16) for i in range(2)], axis=1
        )
        lifted = dot(liftw[...], scaled)
        for i in range(2):
            feats0[2 * p + i] = modulate(lifted[:, i * lon : (i + 1) * lon], 0, core).astype(BF16)
    pl.semaphore_wait(barrier, n_hor - 1 + n_near * (1 + core))
    even = lax.rem(lat, 2) == 0
    send_order = [(0, even), (1, lat >= 0), (0, jnp.logical_not(even))]
    for side, when in send_order:

        @pl.when(has(side) & when)
        def _():
            first_halo(side, core).start()

    sig_copy.start()
    x_copy.start()
    ret_copy.start()
    cur_copy.start()
    pooled = jnp.zeros((hidden, lon), F32)
    for first in (0, 2):
        flat = [feats0[first + 4 * g + r] for g in range(2) for r in range(2)]
        pooled = pooled + dot(jnp.concatenate(flat, axis=1), poolm[...])
    pooled = packed(pooled)
    qsend[0] = pooled.astype(WIRE)
    psend[0, core] = pooled
    psend[0, other] = jnp.zeros((half, lon), F32)
    send_far_pool(0)
    pool_copy(0).start()
    rate[core] = packed_rate(rets[core])
    for d in range(1, n_chip):
        for to in range(2):

            @pl.when(chip + d < n_chip)
            def _():
                far_rate_copy(d, to, core).start()

    for load in loads[7:]:
        load.wait()
    taps[...] = jnp.concatenate([convw[a] for a in range(3)], axis=1)

    for c in range(2):

        @pl.when(core == c)
        def _():
            row_of = outer_row if c else inner_row
            for g in range(2):
                for r in range(2):
                    place(feats0[row_of(g, r)].astype(F32), c, g, r)
                frecv[0, g, c] = feats0[(2 + g * (rows - 5)) if c else (1 + g * (rows - 3))]
            convolve(c, c, 0)
            remote(sig.at[1 - c], sig.at[1 - c], l_sem.at[2], g_sem.at[0], partner).wait_recv()
            set_modulation(0, 1 - c)
            x_copy.wait_recv()
            for p in range(3):
                got = jnp.concatenate([xrecv[2 * p], xrecv[2 * p + 1]], axis=1)
                lifted = dot(liftw[...], got)
                for i in range(2):
                    feat = modulate(lifted[:, i * lon : (i + 1) * lon], 0, 1 - c)
                    if p < 2:
                        place(feat, 1 - c, p, i)
                    else:
                        frecv[0, i, 1 - c] = feat.astype(BF16)
            convolve(1 - c, c, 0)

    remote(rets.at[other], rets.at[other], l_sem.at[3], g_sem.at[1], partner).wait_recv()
    rate[other] = packed_rate(rets[other])
    remote(csend, cur.at[other], l_sem.at[4], g_sem.at[2], partner).wait_recv()
    for copy in (sig_copy, ret_copy, cur_copy, x_copy):
        copy.wait_send()
    for side in range(2):

        @pl.when(has(side))
        def _():
            first_halo(side, core).wait_send()

    def far_rates():
        for d in range(1, n_chip):

            @pl.when(chip >= d)
            def _():
                for c in range(2):
                    far_rate_copy(d, 0, c).wait_recv()
                second = packed_rate(rfar[d - 1, 1])
                raw_rate[d - 1] = second
                if d < n_chip - 1:
                    pair = packed_rate(rfar[d - 1, 0]) * second
                    coef[d] = pair if d == 1 else coef[d - 1] * pair

    def step(s, final):
        keep, gain, scale_next = [], [], []
        for f in range(2):
            now, after = sig[f, pl.ds(s, 1), :], sig[f, pl.ds(s + 1, 1), :]
            ratio = after / now
            keep.append(ratio + (1.0 - ratio) / (now * now + 1.0))
            gain.append((1.0 - ratio) * (now * in_scale_of(now)))
            scale_next.append(in_scale_of(after))

        if not final:

            @pl.when((s == STEPS - 2) & (chip > 0))
            def _():
                last, end = sig[0, pl.ds(s + 1, 1), :], sig[0, pl.ds(s + 2, 1), :]
                hold = keep[0] * (end / last + (1.0 - end / last) / (last * last + 1.0))
                for g in range(2):
                    for r in range(2):
                        base_send[g, r, 0:chans, :] = (hold * cur[0, g, r]).astype(BF16)
                base_copy(core).start()

        def await_feats():
            @pl.when(s > 0)
            def _():
                feat_copy(s).wait_recv()

        def joint_edges(c):
            for g in range(2):
                j = joint(g, c)
                rhs = [shifted(frecv[s, g, f].astype(F32)) for f in range(2)]
                extra = dot(convw[2 * j], jnp.concatenate(rhs, axis=1))
                for f in range(2):
                    acc[f][g, j] += extra[:, f * lon : (f + 1) * lon]

        def await_halos():
            for side in range(2):
                if not final:

                    @pl.when(has(side) & (s == 0))
                    def _():
                        for f in range(2):
                            first_halo(1 - side, f).wait_recv()

                @pl.when(has(side) & (s > 0))
                def _():
                    halo_copy(s, 1 - side).wait_recv()

        def remote_edges(frames):
            near = [hrecv[s, side, f, 0:chans, :] for side in range(2) for f in frames]
            near = dot(liftw[...], jnp.concatenate(near, axis=1))
            for side in range(2):
                rhs = []
                for i, f in enumerate(frames):
                    at = (side * len(frames) + i) * lon
                    feat = modulate(near[:, at : at + lon], s, f)
                    rhs.append(shifted(jnp.where(has(side), feat, 0.0)))
                extra = dot(convw[2 * side], jnp.concatenate(rhs, axis=1))
                for i, f in enumerate(frames):
                    acc[f][side, side] += extra[:, i * lon : (i + 1) * lon]

        def await_pools():
            if not final:

                @pl.when(s == 0)
                def _():
                    far_rates()

            pool_copy(s).wait_recv()
            for d in range(1, n_chip):
                for c in range(2):

                    @pl.when(chip >= d)
                    def _():
                        far_pool_wait(s, d, c).wait_recv()

        def contexts():
            first = psend[s, 0] + precv[s, 0]
            if n_chip > 1:
                total = jnp.zeros((half, lon), F32)
                for d in range(1, n_chip):
                    got = qrecv[s, d - 1, 0].astype(F32)
                    if not final:
                        got = got * jnp.where(s == 0, raw_rate[d - 1], 1.0)
                    got = got + qrecv[s, d - 1, 1].astype(F32)
                    got = got if d == 1 else coef[d - 1] * got
                    total = total + jnp.where(chip >= d, got, 0.0)
                first = first + rate[0] * total
            second = rate[1] * first + (psend[s, 1] + precv[s, 1])
            both = []
            for total in (first, second):
                high = total.astype(BF16)
                both.append(jnp.concatenate([high, (total - high.astype(F32)).astype(BF16)], axis=1))
            both = jnp.concatenate(both, axis=0)
            for side in range(2):
                wide = dot(both, spread[side])
                for f in range(2):
                    for tok in range(2):
                        up[f, tok, side * half : (side + 1) * half, :] = wide[
                            f * half : (f + 1) * half, tok * lon : (tok + 1) * lon
                        ]

        def finish(cells):
            gated = []
            for f, g, r in cells:
                feat = feature(f, g, r).astype(F32)
                gated.append(half_silu(0.5 * (feat + acc[f][g, r] + up[f, g])).astype(BF16))
            outputs = dot(outw[...], jnp.concatenate(gated, axis=1))
            for i, (f, g, r) in enumerate(cells):
                nxt = keep[f] * cur[f, g, r] + gain[f] * outputs[:, i * lon : (i + 1) * lon]
                cur[f, g, r] = nxt
                if g == r and not final:
                    hsend[s + 1, g, f, 0:chans, :] = (nxt * scale_next[f]).astype(BF16)
                if f == 0 and final:
                    rest_send[1 if g == r else 0, g, 0:chans, :] = (
                        nxt - base_send[g, r, 0:chans, :].astype(F32)
                    ).astype(BF16)

        def send_rest(copy):
            @pl.when(chip > 0)
            def _():
                copy.start()

        def lift(pairs):
            for pair in pairs:
                f = pair[0][0]
                scaled = jnp.concatenate(
                    [(cur[cell] * scale_next[f]).astype(BF16) for cell in pair], axis=1
                )
                lifted = dot(liftw[...], scaled)
                for i, cell in enumerate(pair):
                    place(modulate(lifted[:, i * lon : (i + 1) * lon], s + 1, f), *cell)

        def send_feats(c):
            @pl.when(s > 0)
            def _():
                feat_copy(s).wait_send()

            for f in range(2):
                for g in range(2):
                    fsend[s + 1, g, f] = feature(f, g, joint(g, c))
            feat_copy(s + 1).start()

        def send_pools():
            pooled = None
            for cells in (near_cells, edge_cells):
                flat = [jnp.concatenate([feature(*cell) for cell in cells[f]], axis=1) for f in range(2)]
                part = dot(jnp.concatenate(flat, axis=0), poolm[lon : 3 * lon, :])
                pooled = part if pooled is None else pooled + part
            first, second = (packed(pooled[f * hidden : (f + 1) * hidden]) for f in range(2))
            qsend[s + 1] = (rate[1] * first + second).astype(WIRE)
            drain_far_pool(s)
            send_far_pool(s + 1)
            psend[s + 1, 0] = first
            psend[s + 1, 1] = second
            pool_copy(s).wait_send()
            pool_copy(s + 1).start()

        near_cells = [[(f, 0, 1), (f, 1, 0)] for f in range(2)]
        edge_cells = [[(f, 0, 0), (f, 1, 1)] for f in range(2)]

        def send_edges():
            for side, when in send_order:

                @pl.when(has(side) & when & (s > 0))
                def _():
                    halo_copy(s, side).wait_send()

                @pl.when(has(side) & when)
                def _():
                    halo_copy(s + 1, side).start()

        all_near, all_edge = near_cells[0] + near_cells[1], edge_cells[0] + edge_cells[1]

        def lift_near():
            for f in range(2):
                set_modulation(s + 1, f)
            lift(near_cells)
            send_feats(1)

        @pl.when(outer)
        def _():
            await_pools()
            contexts()
            finish(all_near)
            if final:
                send_rest(outer_rest(0))

            if not final:

                @pl.when(chip == 0)
                def _():
                    lift_near()

            await_halos()
            remote_edges([0, 1])
            finish(all_edge)
            if final:
                send_rest(outer_rest(1))
                feat_copy(s).wait_send()
            else:
                send_edges()

            if final:
                for f in range(2):
                    final_copy(f).start()
            else:

                @pl.when(chip > 0)
                def _():
                    lift_near()

                lift(edge_cells)
                send_pools()
                feat_copy(s + 1).wait_recv()
                for f in range(2):
                    convolve(f, 1, s + 1)

        @pl.when(jnp.logical_not(outer))
        def _():
            await_feats()
            joint_edges(0)
            await_pools()
            contexts()
            if final:
                finish(near_cells[0] + edge_cells[0])
                send_rest(inner_rest)
                feat_copy(s).wait_send()
                finish(near_cells[1] + edge_cells[1])
                final_copy(1).start()
            else:
                finish(near_cells[0] + edge_cells[0])
                finish(near_cells[1] + edge_cells[1])
                for f in range(2):
                    set_modulation(s + 1, f)
                lift(edge_cells)
                send_feats(0)
                lift(near_cells)
                send_pools()
                for f in range(2):
                    convolve(f, 0, s + 1)

    @pl.loop(0, STEPS - 1)
    def _(s):
        step(s, False)

    step(STEPS - 1, True)

    def put(out, row, value):
        out[pl.ds(row, chans, stride=rows), :] = value

    cells = [(g, r) for g in range(2) for r in range(2)]

    @pl.when(outer)
    def _():
        for g, r in cells:
            put(wout, outer_row(g, r), cur[1, g, r])

        final_copy(1).wait_recv()
        for g, r in cells:
            put(wout, inner_row(g, r), fin_recv[1, g, r])

        @pl.when(chip == n_chip - 1)
        def _():
            fresh_load.wait()
            arr[...] = plan[plan.shape[0] - 1] * arr[...]

        @pl.when(chip < n_chip - 1)
        def _():
            for c in range(2):
                base_copy(c).wait_recv()
            inner_rest.wait_recv()
            for c, stage in ((0, 0), (0, 1), (1, 0), (1, 1)):
                if c:
                    outer_rest(stage).wait_recv()
                for g in range(2):
                    r = g if stage else 1 - g
                    row = outer_row(g, r) if c else inner_row(g, r)
                    value = base_recv[c, g, r, 0:chans, :].astype(F32)
                    put(arr, row, value + rest_recv[c, stage, g, 0:chans, :].astype(F32))

    @pl.when(jnp.logical_not(outer))
    def _():
        for g, r in cells:
            put(wout, inner_row(g, r), cur[0, g, r])
            put(arr, inner_row(g, r), cur[1, g, r])
        for f, out in ((1, arr), (0, wout)):
            final_copy(f).wait_recv()
            for g, r in cells:
                put(out, outer_row(g, r), fin_recv[f, g, r])

    final_copy(1).wait_send()
    pool_copy(STEPS - 1).wait_send()
    drain_far_pool(STEPS - 1)
    for d in range(1, n_chip):
        for to in range(2):

            @pl.when(chip + d < n_chip)
            def _():
                far_rate_copy(d, to, core).wait_send()

    for side in range(2):

        @pl.when(outer & has(side))
        def _():
            halo_copy(STEPS - 1, side).wait_send()

    @pl.when(outer)
    def _():
        final_copy(0).wait_send()

    @pl.when(chip > 0)
    def _():
        base_copy(core).wait_send()

    @pl.when((chip > 0) & outer)
    def _():
        for stage in range(2):
            outer_rest(stage).wait_send()

    @pl.when((chip > 0) & jnp.logical_not(outer))
    def _():
        inner_rest.wait_send()


def write(a, b, a_out, b_out, sem):
    copies = [pltpu.make_async_copy(x, y, sem.at[i]) for i, (x, y) in enumerate([(a, a_out), (b, b_out)])]
    for copy in copies:
        copy.start()
    for copy in copies:
        copy.wait()


def body(
    n_hor,
    n_lat,
    window,
    fresh_noise,
    level_index,
    plan,
    retention,
    lift_weight,
    mod_scale,
    mod_shift,
    conv_weight,
    out_weight,
):
    frames, chans, rows, lon = window.shape
    hidden = conv_weight.shape[1]
    half = hidden // 2
    cpad = -(-chans // 8) * 8
    n_chip = n_hor // 2
    peers = max(1, n_chip - 1)
    vmem = pl.BlockSpec(memory_space=pltpu.VMEM)
    hbm = pl.BlockSpec(memory_space=pltpu.HBM)
    flat = jax.ShapeDtypeStruct((chans * rows, lon), F32)
    dma = pltpu.SemaphoreType.DMA
    current, arriving = pl.pallas_call(
        functools.partial(kernel, rows, lon, n_hor, n_lat),
        out_shape=(pltpu.VMEM(flat.shape, F32), pltpu.VMEM(flat.shape, F32)),
        in_specs=[hbm] * 10,
        out_specs=(vmem, vmem),
        scratch_shapes=[
            pltpu.SMEM(level_index.shape, jnp.int32),
            pltpu.SMEM(plan.shape, F32),
            pltpu.VMEM((chans * rows, lon), F32),
            pltpu.VMEM((2, 1, hidden), F32),
            pltpu.VMEM((peers, 2, 1, hidden), F32),
            pltpu.VMEM((1, hidden), F32),
            pltpu.VMEM((1, hidden), F32),
            pltpu.VMEM((chans, hidden), BF16),
            pltpu.VMEM(conv_weight.shape, BF16),
            pltpu.VMEM((chans, hidden), BF16),
            pltpu.VMEM((hidden, chans), BF16),
            pltpu.VMEM((hidden, 9 * hidden), BF16),
            pltpu.VMEM((rows, chans, lon), F32),
            pltpu.VMEM((rows, hidden, lon), BF16),
            pltpu.VMEM((2, 2, chans, lon), F32),
            pltpu.VMEM((6, chans, lon), BF16),
            pltpu.VMEM((6, chans, lon), BF16),
            pltpu.VMEM((2, 2, 2, chans, lon), F32),
            pltpu.VMEM((8, 3 * hidden, lon), BF16),
            pltpu.VMEM((8, 3 * hidden, lon), BF16),
            pltpu.VMEM((STEPS, 2, 2, hidden, lon), BF16),
            pltpu.VMEM((STEPS, 2, 2, hidden, lon), BF16),
            pltpu.VMEM((2, 2, hidden, lon), F32),
            pltpu.VMEM((2, 2, hidden, lon), F32),
            pltpu.VMEM((2, 2, hidden, lon), F32),
            pltpu.VMEM((2, hidden, lon), F32),
            pltpu.VMEM((2, 2, 2, hidden, lon), F32),
            pltpu.VMEM((2, 8, lon), F32),
            pltpu.VMEM((4 * lon, lon), BF16),
            pltpu.VMEM((2, 2 * lon, 2 * lon), BF16),
            pltpu.VMEM((2, half, lon), F32),
            pltpu.VMEM((peers, half, lon), F32),
            pltpu.VMEM((peers, half, lon), F32),
            pltpu.VMEM((STEPS + 1, 2, 2, cpad, lon), BF16),
            pltpu.VMEM((STEPS, 2, 2, cpad, lon), BF16),
            pltpu.VMEM((STEPS, 2, half, lon), F32),
            pltpu.VMEM((STEPS, 2, half, lon), F32),
            pltpu.VMEM((STEPS, half, lon), WIRE),
            pltpu.VMEM((STEPS, peers, 2, half, lon), WIRE),
            pltpu.VMEM((2, 2, cpad, lon), BF16),
            pltpu.VMEM((2, 2, 2, cpad, lon), BF16),
            pltpu.VMEM((2, 2, cpad, lon), BF16),
            pltpu.VMEM((2, 2, 2, cpad, lon), BF16),
            pltpu.VMEM((2, 2, 2, chans, lon), F32),
            dma((10,)),
            dma((4,)),
            dma((3, 2)),
            dma((2,)),
            dma((3,)),
            dma((peers, 2)),
            dma((STEPS, peers, 2)),
            dma((peers, 2)),
            dma((peers, 2)),
            dma((5,)),
            dma((2,)),
        ],
        compiler_params=pltpu.CompilerParams(
            collective_id=0, has_side_effects=True, vmem_limit_bytes=66400000
        ),
    )(
        level_index,
        plan,
        window.reshape(chans * rows, lon),
        fresh_noise.reshape(chans * rows, lon),
        retention,
        mod_scale.reshape(1, hidden),
        mod_shift.reshape(1, hidden),
        lift_weight.T,
        conv_weight,
        out_weight,
    )
    shape = (frames, chans, rows, lon)
    current, rolled = pl.pallas_call(
        write,
        out_shape=(flat, flat),
        in_specs=[vmem, vmem],
        out_specs=(hbm, hbm),
        scratch_shapes=[dma((2,))],
        compiler_params=pltpu.CompilerParams(vmem_limit_bytes=4 * 1024 * 1024),
    )(current, arriving)
    return (current.reshape(shape), rolled.reshape(shape))


def solution(mesh):
    in_specs = (
        P("hor", None, "lat", None),
        P(None, "lat", None),
        P("hor"),
        P(),
        P("hor", None),
        P(),
        P(),
        P(),
        P(),
        P(),
    )
    out_specs = (P("hor", None, "lat", None), P("hor", None, "lat", None))
    run = functools.partial(body, mesh.shape["hor"], mesh.shape["lat"])
    return jax.shard_map(run, mesh=mesh, in_specs=in_specs, out_specs=out_specs, check_vma=False)
```

```python
import functools

import jax
import jax.numpy as jnp
from jax import lax
from jax.experimental import pallas as pl
from jax.experimental.pallas import tpu as pltpu
from jax.sharding import PartitionSpec as P

POOL = 4
STEPS = 3
MESH = pl.DeviceIdType.MESH
F32 = jnp.float32
BF16 = jnp.bfloat16
WIRE = jnp.bfloat16


def dot(a, b):
    return jnp.dot(a, b, preferred_element_type=F32)


def kernel(
    rows,
    lon,
    n_hor,
    n_lat,
    lvl_h,
    plan_h,
    win_h,
    fresh_h,
    ret_h,
    msc_h,
    msh_h,
    lift_h,
    convw_h,
    outw_h,
    wout,
    arr,
    lvl,
    plan,
    win,
    rets,
    rfar,
    msc,
    msh,
    liftt,
    convw,
    outw,
    liftw,
    taps,
    home,
    feats0,
    csend,
    xsend,
    xrecv,
    cur,
    stack_a,
    stack_b,
    fsend,
    frecv,
    acc_a,
    acc_b,
    up,
    mods,
    smsh,
    sig,
    poolm,
    spread,
    rate,
    coef,
    raw_rate,
    hsend,
    hrecv,
    psend,
    precv,
    qsend,
    qrecv,
    base_send,
    base_recv,
    rest_send,
    rest_recv,
    fin_recv,
    l_sem,
    g_sem,
    h_sem,
    f_sem,
    p_sem,
    q_ssem,
    q_rsem,
    rf_ssem,
    rf_rsem,
    r_sem,
    e_sem,
):
    hidden, chans = liftw.shape
    half = hidden // 2
    n_chip = n_hor // 2
    stack, acc = (stack_a, stack_b), (acc_a, acc_b)
    hor = lax.axis_index("hor")
    lat = lax.axis_index("lat")
    chip = hor // 2
    core = lax.rem(hor, 2)
    other = 1 - core
    outer = core == 1
    partner = {"hor": hor + 1 - 2 * core}
    n_near = jnp.where(lat > 0, 1, 0) + jnp.where(lat < n_lat - 1, 1, 0)

    def has(side):
        return lat > 0 if side == 0 else lat < n_lat - 1

    def remote(src, dst, ssem, rsem, where):
        return pltpu.make_async_remote_copy(
            src_ref=src,
            dst_ref=dst,
            send_sem=ssem,
            recv_sem=rsem,
            device_id=where,
            device_id_type=MESH,
        )

    barrier = pltpu.get_barrier_semaphore()

    def greet(where):
        pl.semaphore_signal(barrier, inc=1, device_id=where, device_id_type=MESH)

    for side in range(2):
        near = lat - 1 + 2 * side

        @pl.when(has(side))
        def _():
            greet({"hor": 2 * chip + 1, "lat": near})

        @pl.when(has(side) & outer)
        def _():
            greet({"hor": 2 * chip, "lat": near})

    for d in range(1, n_hor):
        greet({"hor": lax.rem(hor + d, n_hor)})

    pairs = [(lift_h, liftt), (lvl_h, lvl), (plan_h, plan)]
    pairs += [(msc_h, msc), (msh_h, msh), (ret_h, rets.at[core]), (win_h, win)]
    pairs += [(convw_h, convw), (outw_h, outw)]
    loads = [pltpu.make_async_copy(a, b, l_sem.at[i]) for i, (a, b) in enumerate(pairs)]
    fresh_load = pltpu.make_async_copy(fresh_h, arr, l_sem.at[len(pairs)])
    for load in loads:
        load.start()

    @pl.when(hor == n_hor - 1)
    def _():
        fresh_load.start()

    for side in range(2):

        @pl.when(outer & jnp.logical_not(has(side)))
        def _():
            hrecv[:, side] = jnp.zeros_like(hrecv[:, side])

    for f in range(2):
        for block in (0, 5):
            stack[f][block] = jnp.zeros_like(stack[f][block])

    def column(row_ref_value, start, count):
        sub = lax.broadcasted_iota(jnp.int32, (count, hidden), 0) + start
        lane = lax.broadcasted_iota(jnp.int32, (count, hidden), 1)
        return jnp.sum(jnp.where(sub == lane, row_ref_value, 0.0), axis=1, keepdims=True)

    def packed_rate(value):
        lane = lax.broadcasted_iota(jnp.int32, (half, lon), 1)
        lo = jnp.broadcast_to(column(value, 0, half), (half, lon))
        hi = jnp.broadcast_to(column(value, half, half), (half, lon))
        return jnp.where(lane < lon // 2, lo, hi)

    groups = lon // POOL
    shift = POOL.bit_length() - 1
    k = lax.broadcasted_iota(jnp.int32, (4 * lon, lon), 0)
    n = lax.broadcasted_iota(jnp.int32, (4 * lon, lon), 1)
    want = lax.shift_right_logical(k, lon.bit_length()) * groups + lax.shift_right_logical(
        lax.bitwise_and(k, lon - 1), shift
    )
    poolm[...] = jnp.where(want == n, 1.0 / (POOL * POOL), 0.0).astype(BF16)
    for side in range(2):
        k = lax.broadcasted_iota(jnp.int32, (2 * lon, 2 * lon), 0)
        n = lax.broadcasted_iota(jnp.int32, (2 * lon, 2 * lon), 1)
        want = side * (lon // 2) + lax.shift_right_logical(n, shift)
        spread[side] = jnp.where(lax.bitwise_and(k, lon - 1) == want, 1.0, 0.0).astype(BF16)

    def in_scale_of(now):
        return 1.0 / jnp.sqrt(now * now + 1.0)

    def outer_row(g, r):
        return g * (rows - 2) + r

    def inner_row(g, r):
        return 2 + 2 * g + r

    def my_row(g, r):
        return jnp.where(outer, outer_row(g, r), inner_row(g, r))

    def their_row(g, r):
        return jnp.where(outer, inner_row(g, r), outer_row(g, r))

    def joint(g, c):
        return 1 - g if c else g

    sig_copy = remote(sig.at[core], sig.at[core], l_sem.at[2], g_sem.at[0], partner)
    ret_copy = remote(rets.at[core], rets.at[core], l_sem.at[3], g_sem.at[1], partner)
    cur_copy = remote(csend, cur.at[core], l_sem.at[4], g_sem.at[2], partner)
    x_copy = remote(xsend, xrecv, l_sem.at[5], g_sem.at[3], partner)

    def beside(side):
        return {"hor": 2 * chip + 1, "lat": lat - 1 + 2 * side}

    def first_halo(side, f):
        return remote(
            hsend.at[0, side, f],
            hrecv.at[0, 1 - side, f],
            l_sem.at[side],
            h_sem.at[f, 1 - side],
            beside(side),
        )

    def halo_copy(s, side):
        return remote(
            hsend.at[s, side],
            hrecv.at[s, 1 - side],
            l_sem.at[side],
            h_sem.at[2 * lax.rem(s, 2), 1 - side],
            beside(side),
        )

    def feat_copy(s):
        return remote(fsend.at[s], frecv.at[s], l_sem.at[6], f_sem.at[lax.rem(s, 2)], partner)

    def pool_copy(s):
        return remote(psend.at[s], precv.at[s], l_sem.at[7], p_sem.at[lax.rem(s, 2)], partner)

    def far_pool_copy(s, d, to):
        return remote(
            qsend.at[s],
            qrecv.at[s, d - 1, core],
            q_ssem.at[d - 1, to],
            q_rsem.at[s, d - 1, core],
            {"hor": 2 * (chip + d) + to},
        )

    def far_pool_wait(s, d, c):
        return remote(
            qsend.at[s],
            qrecv.at[s, d - 1, c],
            q_ssem.at[d - 1, 0],
            q_rsem.at[s, d - 1, c],
            {"hor": 2 * chip + c},
        )

    def far_rate_copy(d, to, c):
        return remote(
            rets.at[core],
            rfar.at[d - 1, c],
            rf_ssem.at[d - 1, to],
            rf_rsem.at[d - 1, c],
            {"hor": 2 * (chip + d) + to},
        )

    back = {"hor": 2 * chip - 1}

    def base_copy(c):
        return remote(base_send, base_recv.at[c], l_sem.at[2], r_sem.at[c], back)

    def outer_rest(stage):
        return remote(
            rest_send.at[stage],
            rest_recv.at[1, stage],
            l_sem.at[3 + stage],
            r_sem.at[2 + stage],
            back,
        )

    inner_rest = remote(rest_send, rest_recv.at[0], l_sem.at[3], r_sem.at[4], back)

    def final_copy(f):
        return remote(cur.at[f], fin_recv.at[f], l_sem.at[5 + f], e_sem.at[f], partner)

    def half_silu(h):
        return h + h * jnp.tanh(h)

    def shifted(feat):
        ahead = pltpu.roll(feat, 1, 1).astype(BF16)
        behind = pltpu.roll(feat, lon - 1, 1).astype(BF16)
        return jnp.concatenate([ahead, feat.astype(BF16), behind], axis=0)

    low = slice(hidden, 2 * hidden)

    def place(feat, f, g, r):
        stack[f][1 + 2 * g + r] = shifted(feat)

    def feature(f, g, r):
        return stack[f][1 + 2 * g + r, low]

    def convolve(f, c, s):
        for g in range(2):
            blocks = [0, 1, 2, 6 if c else 3] if g == 0 else [7 if c else 2, 3, 4, 5]
            if c:
                stack[f][6 + g] = shifted(frecv[s, g, f].astype(F32))
            wide = [
                jnp.concatenate([stack[f][blocks[a]], stack[f][blocks[a + 1]]], axis=1)
                for a in range(3)
            ]
            total = dot(taps[...], jnp.concatenate(wide, axis=0))
            for r in range(2):
                acc[f][g, r] = total[:, r * lon : (r + 1) * lon]

    def packed(value):
        return value[0:half] + pltpu.roll(value[half:hidden], lon // 2, 1)

    def set_modulation(s, f):
        log_sigma = jnp.log(sig[f, pl.ds(s, 1), :])
        smsh[lax.rem(s, 2), f, 0] = 0.5 * (1.0 + log_sigma * mods[0])
        smsh[lax.rem(s, 2), f, 1] = 0.5 * (log_sigma * mods[1])

    def modulate(value, s, f):
        return half_silu(value * smsh[lax.rem(s, 2), f, 0] + smsh[lax.rem(s, 2), f, 1])

    def send_far_pool(s):
        for d in range(1, n_chip):
            for to in range(2):

                @pl.when(chip + d < n_chip)
                def _():
                    far_pool_copy(s, d, to).start()

    def drain_far_pool(s):
        for d in range(1, n_chip):
            for to in range(2):

                @pl.when(chip + d < n_chip)
                def _():
                    far_pool_copy(s, d, to).wait_send()

    for load in loads[0:6]:
        load.wait()
    sub = lax.broadcasted_iota(jnp.int32, (sig.shape[1], lon), 0)
    levels = jnp.ones((sig.shape[1], lon), F32)
    for s in range(STEPS + 1):
        levels = jnp.where(sub == s, plan[jnp.maximum(lvl[0] - s, 0)], levels)
    sig[core] = levels
    scale = in_scale_of(levels[0:1, :])
    mods[0] = jnp.broadcast_to(column(msc[...], 0, hidden), (hidden, lon))
    mods[1] = jnp.broadcast_to(column(msh[...], 0, hidden), (hidden, lon))
    eye = (
        lax.broadcasted_iota(jnp.int32, (chans, chans), 0)
        == lax.broadcasted_iota(jnp.int32, (chans, chans), 1)
    ).astype(F32).astype(BF16)
    liftw[...] = lax.dot_general(
        liftt[...], eye, (((0,), (0,)), ((), ())), preferred_element_type=F32
    ).astype(BF16)
    set_modulation(0, core)
    loads[6].wait()
    for side, row in enumerate((0, rows - 1)):
        edge_row = win[pl.ds(row, chans, stride=rows), :]
        hsend[0, side, core, 0:chans, :] = (edge_row * scale).astype(BF16)
    for row in range(rows):
        home[row] = win[pl.ds(row, chans, stride=rows), :]
    for g in range(2):
        for r in range(2):
            csend[g, r] = home[their_row(g, r)]
            cur[core, g, r] = home[my_row(g, r)]
            xsend[2 * g + r] = (csend[g, r] * scale).astype(BF16)
        joint_row = jnp.where(outer, 1 + g * (rows - 3), 2 + g * (rows - 5))
        xsend[4 + g] = (home[joint_row] * scale).astype(BF16)
    for p in range(rows // 2):
        scaled = jnp.concatenate(
            [(home[2 * p + i] * scale).astype(BF16) for i in range(2)], axis=1
        )
        lifted = dot(liftw[...], scaled)
        for i in range(2):
            feats0[2 * p + i] = modulate(lifted[:, i * lon : (i + 1) * lon], 0, core).astype(BF16)
    rate[core] = packed_rate(rets[core])
    for load in loads[7:]:
        load.wait()
    taps[...] = jnp.concatenate([convw[a] for a in range(3)], axis=1)
    pl.semaphore_wait(barrier, n_hor - 1 + n_near * (1 + core))
    even = lax.rem(lat, 2) == 0
    send_order = [(0, even), (1, lat >= 0), (0, jnp.logical_not(even))]
    for side, when in send_order:

        @pl.when(has(side) & when)
        def _():
            first_halo(side, core).start()

    sig_copy.start()
    x_copy.start()
    ret_copy.start()
    cur_copy.start()
    pooled = jnp.zeros((hidden, lon), F32)
    for first in (0, 2):
        flat = [feats0[first + 4 * g + r] for g in range(2) for r in range(2)]
        pooled = pooled + dot(jnp.concatenate(flat, axis=1), poolm[...])
    pooled = packed(pooled)
    qsend[0] = pooled.astype(WIRE)
    psend[0, core] = pooled
    psend[0, other] = jnp.zeros((half, lon), F32)
    send_far_pool(0)
    pool_copy(0).start()
    for d in range(1, n_chip):
        for to in range(2):

            @pl.when(chip + d < n_chip)
            def _():
                far_rate_copy(d, to, core).start()


    for c in range(2):

        @pl.when(core == c)
        def _():
            row_of = outer_row if c else inner_row
            for g in range(2):
                for r in range(2):
                    place(feats0[row_of(g, r)].astype(F32), c, g, r)
                frecv[0, g, c] = feats0[(2 + g * (rows - 5)) if c else (1 + g * (rows - 3))]
            convolve(c, c, 0)
            remote(sig.at[1 - c], sig.at[1 - c], l_sem.at[2], g_sem.at[0], partner).wait_recv()
            set_modulation(0, 1 - c)
            x_copy.wait_recv()
            for p in range(3):
                got = jnp.concatenate([xrecv[2 * p], xrecv[2 * p + 1]], axis=1)
                lifted = dot(liftw[...], got)
                for i in range(2):
                    feat = modulate(lifted[:, i * lon : (i + 1) * lon], 0, 1 - c)
                    if p < 2:
                        place(feat, 1 - c, p, i)
                    else:
                        frecv[0, i, 1 - c] = feat.astype(BF16)
            convolve(1 - c, c, 0)

    remote(rets.at[other], rets.at[other], l_sem.at[3], g_sem.at[1], partner).wait_recv()
    rate[other] = packed_rate(rets[other])
    remote(csend, cur.at[other], l_sem.at[4], g_sem.at[2], partner).wait_recv()
    for copy in (sig_copy, ret_copy, cur_copy, x_copy):
        copy.wait_send()
    for side in range(2):

        @pl.when(has(side))
        def _():
            first_halo(side, core).wait_send()

    def far_rates():
        for d in range(1, n_chip):

            @pl.when(chip >= d)
            def _():
                for c in range(2):
                    far_rate_copy(d, 0, c).wait_recv()
                second = packed_rate(rfar[d - 1, 1])
                raw_rate[d - 1] = second
                if d < n_chip - 1:
                    pair = packed_rate(rfar[d - 1, 0]) * second
                    coef[d] = pair if d == 1 else coef[d - 1] * pair

    def step(s, final):
        keep, gain, scale_next = [], [], []
        for f in range(2):
            now, after = sig[f, pl.ds(s, 1), :], sig[f, pl.ds(s + 1, 1), :]
            ratio = after / now
            keep.append(ratio + (1.0 - ratio) / (now * now + 1.0))
            gain.append((1.0 - ratio) * (now * in_scale_of(now)))
            scale_next.append(in_scale_of(after))

        if not final:

            @pl.when((s == STEPS - 2) & (chip > 0))
            def _():
                last, end = sig[0, pl.ds(s + 1, 1), :], sig[0, pl.ds(s + 2, 1), :]
                hold = keep[0] * (end / last + (1.0 - end / last) / (last * last + 1.0))
                for g in range(2):
                    for r in range(2):
                        base_send[g, r, 0:chans, :] = (hold * cur[0, g, r]).astype(BF16)
                base_copy(core).start()

        def await_feats():
            @pl.when(s > 0)
            def _():
                feat_copy(s).wait_recv()

        def joint_edges(c):
            for g in range(2):
                j = joint(g, c)
                rhs = [shifted(frecv[s, g, f].astype(F32)) for f in range(2)]
                extra = dot(convw[2 * j], jnp.concatenate(rhs, axis=1))
                for f in range(2):
                    acc[f][g, j] += extra[:, f * lon : (f + 1) * lon]

        def await_halos():
            for side in range(2):
                if not final:

                    @pl.when(has(side) & (s == 0))
                    def _():
                        for f in range(2):
                            first_halo(1 - side, f).wait_recv()

                @pl.when(has(side) & (s > 0))
                def _():
                    halo_copy(s, 1 - side).wait_recv()

        def remote_edges(frames):
            sides = []
            for side in range(2):
                near = [hrecv[s, side, f, 0:chans, :] for f in frames]
                near = dot(liftw[...], jnp.concatenate(near, axis=1))
                sides.append([])
                for i, f in enumerate(frames):
                    feat = modulate(near[:, i * lon : (i + 1) * lon], s, f)
                    sides[side].append(shifted(jnp.where(has(side), feat, 0.0)))
            for side in range(2):
                extra = dot(convw[2 * side], jnp.concatenate(sides[side], axis=1))
                for i, f in enumerate(frames):
                    acc[f][side, side] += extra[:, i * lon : (i + 1) * lon]

        def await_pools():
            if not final:

                @pl.when(s == 0)
                def _():
                    far_rates()

            pool_copy(s).wait_recv()
            for d in range(1, n_chip):
                for c in range(2):

                    @pl.when(chip >= d)
                    def _():
                        far_pool_wait(s, d, c).wait_recv()

        def contexts():
            first = psend[s, 0] + precv[s, 0]
            if n_chip > 1:
                total = jnp.zeros((half, lon), F32)
                for d in range(1, n_chip):
                    got = qrecv[s, d - 1, 0].astype(F32)
                    if not final:
                        got = got * jnp.where(s == 0, raw_rate[d - 1], 1.0)
                    got = got + qrecv[s, d - 1, 1].astype(F32)
                    got = got if d == 1 else coef[d - 1] * got
                    total = total + jnp.where(chip >= d, got, 0.0)
                first = first + rate[0] * total
            second = rate[1] * first + (psend[s, 1] + precv[s, 1])
            both = []
            for total in (first, second):
                high = total.astype(BF16)
                both.append(jnp.concatenate([high, (total - high.astype(F32)).astype(BF16)], axis=1))
            both = jnp.concatenate(both, axis=0)
            for side in range(2):
                wide = dot(both, spread[side])
                for f in range(2):
                    for tok in range(2):
                        up[f, tok, side * half : (side + 1) * half, :] = wide[
                            f * half : (f + 1) * half, tok * lon : (tok + 1) * lon
                        ]

        def finish(cells):
            gated = []
            for f, g, r in cells:
                feat = feature(f, g, r).astype(F32)
                gated.append(half_silu(0.5 * (feat + acc[f][g, r] + up[f, g])).astype(BF16))
            outputs = dot(outw[...], jnp.concatenate(gated, axis=1))
            for i, (f, g, r) in enumerate(cells):
                nxt = keep[f] * cur[f, g, r] + gain[f] * outputs[:, i * lon : (i + 1) * lon]
                cur[f, g, r] = nxt
                if g == r and not final:
                    hsend[s + 1, g, f, 0:chans, :] = (nxt * scale_next[f]).astype(BF16)
                if f == 0 and final:
                    rest_send[1 if g == r else 0, g, 0:chans, :] = (
                        nxt - base_send[g, r, 0:chans, :].astype(F32)
                    ).astype(BF16)

        def send_rest(copy):
            @pl.when(chip > 0)
            def _():
                copy.start()

        def lift(pairs):
            for pair in pairs:
                f = pair[0][0]
                scaled = jnp.concatenate(
                    [(cur[cell] * scale_next[f]).astype(BF16) for cell in pair], axis=1
                )
                lifted = dot(liftw[...], scaled)
                for i, cell in enumerate(pair):
                    place(modulate(lifted[:, i * lon : (i + 1) * lon], s + 1, f), *cell)

        def send_feats(c):
            @pl.when(s > 0)
            def _():
                feat_copy(s).wait_send()

            for f in range(2):
                for g in range(2):
                    fsend[s + 1, g, f] = feature(f, g, joint(g, c))
            feat_copy(s + 1).start()

        def send_pools():
            pooled = None
            for cells in (near_cells, edge_cells):
                flat = [jnp.concatenate([feature(*cell) for cell in cells[f]], axis=1) for f in range(2)]
                part = dot(jnp.concatenate(flat, axis=0), poolm[lon : 3 * lon, :])
                pooled = part if pooled is None else pooled + part
            first, second = (packed(pooled[f * hidden : (f + 1) * hidden]) for f in range(2))
            qsend[s + 1] = (rate[1] * first + second).astype(WIRE)
            drain_far_pool(s)
            send_far_pool(s + 1)
            psend[s + 1, 0] = first
            psend[s + 1, 1] = second
            pool_copy(s).wait_send()
            pool_copy(s + 1).start()

        near_cells = [[(f, 0, 1), (f, 1, 0)] for f in range(2)]
        edge_cells = [[(f, 0, 0), (f, 1, 1)] for f in range(2)]

        def send_edges():
            for side, when in send_order:

                @pl.when(has(side) & when & (s > 0))
                def _():
                    halo_copy(s, side).wait_send()

                @pl.when(has(side) & when)
                def _():
                    halo_copy(s + 1, side).start()

        all_near, all_edge = near_cells[0] + near_cells[1], edge_cells[0] + edge_cells[1]

        def lift_near():
            for f in range(2):
                set_modulation(s + 1, f)
            lift(near_cells)
            send_feats(1)

        @pl.when(outer)
        def _():
            await_pools()
            contexts()
            finish(all_near)
            if final:
                send_rest(outer_rest(0))

            if not final:

                @pl.when(chip == 0)
                def _():
                    lift_near()

            await_halos()
            remote_edges([0, 1])
            finish(all_edge)
            if final:
                send_rest(outer_rest(1))
                feat_copy(s).wait_send()
            else:
                send_edges()

            if final:
                for f in range(2):
                    final_copy(f).start()
            else:

                @pl.when(chip > 0)
                def _():
                    lift_near()

                lift(edge_cells)
                send_pools()
                feat_copy(s + 1).wait_recv()
                for f in range(2):
                    convolve(f, 1, s + 1)

        @pl.when(jnp.logical_not(outer))
        def _():
            await_feats()
            joint_edges(0)
            await_pools()
            contexts()
            if final:
                finish(near_cells[0] + edge_cells[0])
                send_rest(inner_rest)
                feat_copy(s).wait_send()
                finish(near_cells[1] + edge_cells[1])
                final_copy(1).start()
            else:
                finish(near_cells[0] + edge_cells[0])
                finish(near_cells[1] + edge_cells[1])
                for f in range(2):
                    set_modulation(s + 1, f)
                lift(edge_cells)
                send_feats(0)
                lift(near_cells)
                send_pools()
                for f in range(2):
                    convolve(f, 0, s + 1)

    @pl.loop(0, STEPS - 1)
    def _(s):
        step(s, False)

    step(STEPS - 1, True)

    def put(out, row, value):
        out[pl.ds(row, chans, stride=rows), :] = value

    cells = [(g, r) for g in range(2) for r in range(2)]

    @pl.when(outer)
    def _():
        for g, r in cells:
            put(wout, outer_row(g, r), cur[1, g, r])

        final_copy(1).wait_recv()
        for g, r in cells:
            put(wout, inner_row(g, r), fin_recv[1, g, r])

        @pl.when(chip == n_chip - 1)
        def _():
            fresh_load.wait()
            arr[...] = plan[plan.shape[0] - 1] * arr[...]

        @pl.when(chip < n_chip - 1)
        def _():
            for c in range(2):
                base_copy(c).wait_recv()
            inner_rest.wait_recv()
            for c, stage in ((0, 0), (0, 1), (1, 0), (1, 1)):
                if c:
                    outer_rest(stage).wait_recv()
                for g in range(2):
                    r = g if stage else 1 - g
                    row = outer_row(g, r) if c else inner_row(g, r)
                    value = base_recv[c, g, r, 0:chans, :].astype(F32)
                    put(arr, row, value + rest_recv[c, stage, g, 0:chans, :].astype(F32))

    @pl.when(jnp.logical_not(outer))
    def _():
        for g, r in cells:
            put(wout, inner_row(g, r), cur[0, g, r])
            put(arr, inner_row(g, r), cur[1, g, r])
        for f, out in ((1, arr), (0, wout)):
            final_copy(f).wait_recv()
            for g, r in cells:
                put(out, outer_row(g, r), fin_recv[f, g, r])

    final_copy(1).wait_send()
    pool_copy(STEPS - 1).wait_send()
    drain_far_pool(STEPS - 1)
    for d in range(1, n_chip):
        for to in range(2):

            @pl.when(chip + d < n_chip)
            def _():
                far_rate_copy(d, to, core).wait_send()

    for side in range(2):

        @pl.when(outer & has(side))
        def _():
            halo_copy(STEPS - 1, side).wait_send()

    @pl.when(outer)
    def _():
        final_copy(0).wait_send()

    @pl.when(chip > 0)
    def _():
        base_copy(core).wait_send()

    @pl.when((chip > 0) & outer)
    def _():
        for stage in range(2):
            outer_rest(stage).wait_send()

    @pl.when((chip > 0) & jnp.logical_not(outer))
    def _():
        inner_rest.wait_send()


def write(a, b, a_out, b_out, sem):
    copies = [pltpu.make_async_copy(x, y, sem.at[i]) for i, (x, y) in enumerate([(a, a_out), (b, b_out)])]
    for copy in copies:
        copy.start()
    for copy in copies:
        copy.wait()


def body(
    n_hor,
    n_lat,
    window,
    fresh_noise,
    level_index,
    plan,
    retention,
    lift_weight,
    mod_scale,
    mod_shift,
    conv_weight,
    out_weight,
):
    frames, chans, rows, lon = window.shape
    hidden = conv_weight.shape[1]
    half = hidden // 2
    cpad = -(-chans // 8) * 8
    n_chip = n_hor // 2
    peers = max(1, n_chip - 1)
    vmem = pl.BlockSpec(memory_space=pltpu.VMEM)
    hbm = pl.BlockSpec(memory_space=pltpu.HBM)
    flat = jax.ShapeDtypeStruct((chans * rows, lon), F32)
    dma = pltpu.SemaphoreType.DMA
    current, arriving = pl.pallas_call(
        functools.partial(kernel, rows, lon, n_hor, n_lat),
        out_shape=(pltpu.VMEM(flat.shape, F32), pltpu.VMEM(flat.shape, F32)),
        in_specs=[hbm] * 10,
        out_specs=(vmem, vmem),
        scratch_shapes=[
            pltpu.SMEM(level_index.shape, jnp.int32),
            pltpu.SMEM(plan.shape, F32),
            pltpu.VMEM((chans * rows, lon), F32),
            pltpu.VMEM((2, 1, hidden), F32),
            pltpu.VMEM((peers, 2, 1, hidden), F32),
            pltpu.VMEM((1, hidden), F32),
            pltpu.VMEM((1, hidden), F32),
            pltpu.VMEM((chans, hidden), BF16),
            pltpu.VMEM(conv_weight.shape, BF16),
            pltpu.VMEM((chans, hidden), BF16),
            pltpu.VMEM((hidden, chans), BF16),
            pltpu.VMEM((hidden, 9 * hidden), BF16),
            pltpu.VMEM((rows, chans, lon), F32),
            pltpu.VMEM((rows, hidden, lon), BF16),
            pltpu.VMEM((2, 2, chans, lon), F32),
            pltpu.VMEM((6, chans, lon), BF16),
            pltpu.VMEM((6, chans, lon), BF16),
            pltpu.VMEM((2, 2, 2, chans, lon), F32),
            pltpu.VMEM((8, 3 * hidden, lon), BF16),
            pltpu.VMEM((8, 3 * hidden, lon), BF16),
            pltpu.VMEM((STEPS, 2, 2, hidden, lon), BF16),
            pltpu.VMEM((STEPS, 2, 2, hidden, lon), BF16),
            pltpu.VMEM((2, 2, hidden, lon), F32),
            pltpu.VMEM((2, 2, hidden, lon), F32),
            pltpu.VMEM((2, 2, hidden, lon), F32),
            pltpu.VMEM((2, hidden, lon), F32),
            pltpu.VMEM((2, 2, 2, hidden, lon), F32),
            pltpu.VMEM((2, 8, lon), F32),
            pltpu.VMEM((4 * lon, lon), BF16),
            pltpu.VMEM((2, 2 * lon, 2 * lon), BF16),
            pltpu.VMEM((2, half, lon), F32),
            pltpu.VMEM((peers, half, lon), F32),
            pltpu.VMEM((peers, half, lon), F32),
            pltpu.VMEM((STEPS + 1, 2, 2, cpad, lon), BF16),
            pltpu.VMEM((STEPS, 2, 2, cpad, lon), BF16),
            pltpu.VMEM((STEPS, 2, half, lon), F32),
            pltpu.VMEM((STEPS, 2, half, lon), F32),
            pltpu.VMEM((STEPS, half, lon), WIRE),
            pltpu.VMEM((STEPS, peers, 2, half, lon), WIRE),
            pltpu.VMEM((2, 2, cpad, lon), BF16),
            pltpu.VMEM((2, 2, 2, cpad, lon), BF16),
            pltpu.VMEM((2, 2, cpad, lon), BF16),
            pltpu.VMEM((2, 2, 2, cpad, lon), BF16),
            pltpu.VMEM((2, 2, 2, chans, lon), F32),
            dma((10,)),
            dma((4,)),
            dma((3, 2)),
            dma((2,)),
            dma((2,)),
            dma((peers, 2)),
            dma((STEPS, peers, 2)),
            dma((peers, 2)),
            dma((peers, 2)),
            dma((5,)),
            dma((2,)),
        ],
        compiler_params=pltpu.CompilerParams(
            collective_id=0, has_side_effects=True, vmem_limit_bytes=66400000
        ),
    )(
        level_index,
        plan,
        window.reshape(chans * rows, lon),
        fresh_noise.reshape(chans * rows, lon),
        retention,
        mod_scale.reshape(1, hidden),
        mod_shift.reshape(1, hidden),
        lift_weight.T,
        conv_weight,
        out_weight,
    )
    shape = (frames, chans, rows, lon)
    current, rolled = pl.pallas_call(
        write,
        out_shape=(flat, flat),
        in_specs=[vmem, vmem],
        out_specs=(hbm, hbm),
        scratch_shapes=[dma((2,))],
        compiler_params=pltpu.CompilerParams(vmem_limit_bytes=4 * 1024 * 1024),
    )(current, arriving)
    return (current.reshape(shape), rolled.reshape(shape))


def solution(mesh):
    in_specs = (
        P("hor", None, "lat", None),
        P(None, "lat", None),
        P("hor"),
        P(),
        P("hor", None),
        P(),
        P(),
        P(),
        P(),
        P(),
    )
    out_specs = (P("hor", None, "lat", None), P("hor", None, "lat", None))
    run = functools.partial(body, mesh.shape["hor"], mesh.shape["lat"])
    return jax.shard_map(run, mesh=mesh, in_specs=in_specs, out_specs=out_specs, check_vma=False)
```

```python
import functools

import jax
import jax.numpy as jnp
from jax import lax
from jax.experimental import pallas as pl
from jax.experimental.pallas import tpu as pltpu
from jax.sharding import PartitionSpec as P

POOL = 4
STEPS = 3
MESH = pl.DeviceIdType.MESH
F32 = jnp.float32
BF16 = jnp.bfloat16
WIRE = jnp.bfloat16


def dot(a, b):
    return jnp.dot(a, b, preferred_element_type=F32)


def kernel(
    rows,
    lon,
    n_hor,
    n_lat,
    lvl_h,
    plan_h,
    win_h,
    fresh_h,
    ret_h,
    msc_h,
    msh_h,
    lift_h,
    convw_h,
    outw_h,
    wout,
    arr,
    lvl,
    plan,
    win,
    rets,
    rfar,
    msc,
    msh,
    liftt,
    convw,
    outw,
    liftw,
    taps,
    home,
    feats0,
    csend,
    xsend,
    xrecv,
    cur,
    stack_a,
    stack_b,
    fsend,
    frecv,
    acc_a,
    acc_b,
    up,
    mods,
    smsh,
    sig,
    poolm,
    spread,
    rate,
    coef,
    raw_rate,
    hsend,
    hrecv,
    psend,
    precv,
    qsend,
    qrecv,
    base_send,
    base_recv,
    rest_send,
    rest_recv,
    fin_recv,
    l_sem,
    g_sem,
    h_sem,
    f_sem,
    p_sem,
    q_ssem,
    q_rsem,
    rf_ssem,
    rf_rsem,
    r_sem,
    e_sem,
):
    hidden, chans = liftw.shape
    half = hidden // 2
    n_chip = n_hor // 2
    stack, acc = (stack_a, stack_b), (acc_a, acc_b)
    hor = lax.axis_index("hor")
    lat = lax.axis_index("lat")
    chip = hor // 2
    core = lax.rem(hor, 2)
    other = 1 - core
    outer = core == 1
    partner = {"hor": hor + 1 - 2 * core}
    n_near = jnp.where(lat > 0, 1, 0) + jnp.where(lat < n_lat - 1, 1, 0)

    def has(side):
        return lat > 0 if side == 0 else lat < n_lat - 1

    def remote(src, dst, ssem, rsem, where):
        return pltpu.make_async_remote_copy(
            src_ref=src,
            dst_ref=dst,
            send_sem=ssem,
            recv_sem=rsem,
            device_id=where,
            device_id_type=MESH,
        )

    barrier = pltpu.get_barrier_semaphore()

    def greet(where):
        pl.semaphore_signal(barrier, inc=1, device_id=where, device_id_type=MESH)

    for side in range(2):
        near = lat - 1 + 2 * side

        @pl.when(has(side))
        def _():
            greet({"hor": 2 * chip + 1, "lat": near})

        @pl.when(has(side) & outer)
        def _():
            greet({"hor": 2 * chip, "lat": near})

    for d in range(1, n_hor):
        greet({"hor": lax.rem(hor + d, n_hor)})

    pairs = [(lift_h, liftt), (lvl_h, lvl), (plan_h, plan)]
    pairs += [(msc_h, msc), (msh_h, msh), (ret_h, rets.at[core]), (win_h, win)]
    pairs += [(convw_h, convw), (outw_h, outw)]
    loads = [pltpu.make_async_copy(a, b, l_sem.at[i]) for i, (a, b) in enumerate(pairs)]
    fresh_load = pltpu.make_async_copy(fresh_h, arr, l_sem.at[len(pairs)])
    for load in loads:
        load.start()

    @pl.when(hor == n_hor - 1)
    def _():
        fresh_load.start()

    for side in range(2):

        @pl.when(outer & jnp.logical_not(has(side)))
        def _():
            hrecv[:, side] = jnp.zeros_like(hrecv[:, side])

    for f in range(2):
        for block in (0, 5):
            stack[f][block] = jnp.zeros_like(stack[f][block])

    def column(row_ref_value, start, count):
        sub = lax.broadcasted_iota(jnp.int32, (count, hidden), 0) + start
        lane = lax.broadcasted_iota(jnp.int32, (count, hidden), 1)
        return jnp.sum(jnp.where(sub == lane, row_ref_value, 0.0), axis=1, keepdims=True)

    def packed_rate(value):
        lane = lax.broadcasted_iota(jnp.int32, (half, lon), 1)
        lo = jnp.broadcast_to(column(value, 0, half), (half, lon))
        hi = jnp.broadcast_to(column(value, half, half), (half, lon))
        return jnp.where(lane < lon // 2, lo, hi)

    groups = lon // POOL
    shift = POOL.bit_length() - 1
    k = lax.broadcasted_iota(jnp.int32, (4 * lon, lon), 0)
    n = lax.broadcasted_iota(jnp.int32, (4 * lon, lon), 1)
    want = lax.shift_right_logical(k, lon.bit_length()) * groups + lax.shift_right_logical(
        lax.bitwise_and(k, lon - 1), shift
    )
    poolm[...] = jnp.where(want == n, 1.0 / (POOL * POOL), 0.0).astype(BF16)
    for side in range(2):
        k = lax.broadcasted_iota(jnp.int32, (2 * lon, 2 * lon), 0)
        n = lax.broadcasted_iota(jnp.int32, (2 * lon, 2 * lon), 1)
        want = side * (lon // 2) + lax.shift_right_logical(n, shift)
        spread[side] = jnp.where(lax.bitwise_and(k, lon - 1) == want, 1.0, 0.0).astype(BF16)

    def in_scale_of(now):
        return 1.0 / jnp.sqrt(now * now + 1.0)

    def outer_row(g, r):
        return g * (rows - 2) + r

    def inner_row(g, r):
        return 2 + 2 * g + r

    def my_row(g, r):
        return jnp.where(outer, outer_row(g, r), inner_row(g, r))

    def their_row(g, r):
        return jnp.where(outer, inner_row(g, r), outer_row(g, r))

    def joint(g, c):
        return 1 - g if c else g

    sig_copy = remote(sig.at[core], sig.at[core], l_sem.at[2], g_sem.at[0], partner)
    ret_copy = remote(rets.at[core], rets.at[core], l_sem.at[3], g_sem.at[1], partner)
    cur_copy = remote(csend, cur.at[core], l_sem.at[4], g_sem.at[2], partner)
    x_copy = remote(xsend, xrecv, l_sem.at[5], g_sem.at[3], partner)

    def beside(side):
        return {"hor": 2 * chip + 1, "lat": lat - 1 + 2 * side}

    def first_halo(side, f):
        return remote(
            hsend.at[0, side, f],
            hrecv.at[0, 1 - side, f],
            l_sem.at[side],
            h_sem.at[f, 1 - side],
            beside(side),
        )

    def halo_copy(s, side):
        return remote(
            hsend.at[s, side],
            hrecv.at[s, 1 - side],
            l_sem.at[side],
            h_sem.at[2 * lax.rem(s, 2), 1 - side],
            beside(side),
        )

    def feat_copy(s):
        return remote(fsend.at[s], frecv.at[s], l_sem.at[6], f_sem.at[lax.rem(s, 2)], partner)

    def pool_copy(s):
        return remote(psend.at[s], precv.at[s], p_sem.at[2], p_sem.at[lax.rem(s, 2)], partner)

    def far_pool_copy(s, d, to):
        return remote(
            qsend.at[s],
            qrecv.at[s, d - 1, core],
            q_ssem.at[d - 1, to],
            q_rsem.at[s, d - 1, core],
            {"hor": 2 * (chip + d) + to},
        )

    def far_pool_wait(s, d, c):
        return remote(
            qsend.at[s],
            qrecv.at[s, d - 1, c],
            q_ssem.at[d - 1, 0],
            q_rsem.at[s, d - 1, c],
            {"hor": 2 * chip + c},
        )

    def far_rate_copy(d, to, c):
        return remote(
            rets.at[core],
            rfar.at[d - 1, c],
            rf_ssem.at[d - 1, to],
            rf_rsem.at[d - 1, c],
            {"hor": 2 * (chip + d) + to},
        )

    back = {"hor": 2 * chip - 1}

    def base_copy(c):
        return remote(base_send, base_recv.at[c], l_sem.at[2], r_sem.at[c], back)

    def outer_rest(stage):
        return remote(
            rest_send.at[stage],
            rest_recv.at[1, stage],
            l_sem.at[3 + stage],
            r_sem.at[2 + stage],
            back,
        )

    inner_rest = remote(rest_send, rest_recv.at[0], l_sem.at[3], r_sem.at[4], back)

    def final_copy(f):
        return remote(cur.at[f], fin_recv.at[f], l_sem.at[5 + f], e_sem.at[f], partner)

    def half_silu(h):
        return h + h * jnp.tanh(h)

    def shifted(feat):
        ahead = pltpu.roll(feat, 1, 1).astype(BF16)
        behind = pltpu.roll(feat, lon - 1, 1).astype(BF16)
        return jnp.concatenate([ahead, feat.astype(BF16), behind], axis=0)

    low = slice(hidden, 2 * hidden)

    def place(feat, f, g, r):
        stack[f][1 + 2 * g + r] = shifted(feat)

    def feature(f, g, r):
        return stack[f][1 + 2 * g + r, low]

    def convolve(f, c, s):
        for g in range(2):
            blocks = [0, 1, 2, 6 if c else 3] if g == 0 else [7 if c else 2, 3, 4, 5]
            if c:
                stack[f][6 + g] = shifted(frecv[s, g, f].astype(F32))
            wide = [
                jnp.concatenate([stack[f][blocks[a]], stack[f][blocks[a + 1]]], axis=1)
                for a in range(3)
            ]
            total = dot(taps[...], jnp.concatenate(wide, axis=0))
            for r in range(2):
                acc[f][g, r] = total[:, r * lon : (r + 1) * lon]

    def packed(value):
        return value[0:half] + pltpu.roll(value[half:hidden], lon // 2, 1)

    def set_modulation(s, f):
        log_sigma = jnp.log(sig[f, pl.ds(s, 1), :])
        smsh[lax.rem(s, 2), f, 0] = 0.5 * (1.0 + log_sigma * mods[0])
        smsh[lax.rem(s, 2), f, 1] = 0.5 * (log_sigma * mods[1])

    def modulate(value, s, f):
        return half_silu(value * smsh[lax.rem(s, 2), f, 0] + smsh[lax.rem(s, 2), f, 1])

    def send_far_pool(s):
        for d in range(1, n_chip):
            for to in range(2):

                @pl.when(chip + d < n_chip)
                def _():
                    far_pool_copy(s, d, to).start()

    def drain_far_pool(s):
        for d in range(1, n_chip):
            for to in range(2):

                @pl.when(chip + d < n_chip)
                def _():
                    far_pool_copy(s, d, to).wait_send()

    for load in loads[0:6]:
        load.wait()
    sub = lax.broadcasted_iota(jnp.int32, (sig.shape[1], lon), 0)
    levels = jnp.ones((sig.shape[1], lon), F32)
    for s in range(STEPS + 1):
        levels = jnp.where(sub == s, plan[jnp.maximum(lvl[0] - s, 0)], levels)
    sig[core] = levels
    scale = in_scale_of(levels[0:1, :])
    mods[0] = jnp.broadcast_to(column(msc[...], 0, hidden), (hidden, lon))
    mods[1] = jnp.broadcast_to(column(msh[...], 0, hidden), (hidden, lon))
    eye = (
        lax.broadcasted_iota(jnp.int32, (chans, chans), 0)
        == lax.broadcasted_iota(jnp.int32, (chans, chans), 1)
    ).astype(F32).astype(BF16)
    liftw[...] = lax.dot_general(
        liftt[...], eye, (((0,), (0,)), ((), ())), preferred_element_type=F32
    ).astype(BF16)
    set_modulation(0, core)
    loads[6].wait()
    for side, row in enumerate((0, rows - 1)):
        edge_row = win[pl.ds(row, chans, stride=rows), :]
        hsend[0, side, core, 0:chans, :] = (edge_row * scale).astype(BF16)
    for row in range(rows):
        home[row] = win[pl.ds(row, chans, stride=rows), :]
    for g in range(2):
        for r in range(2):
            csend[g, r] = home[their_row(g, r)]
            cur[core, g, r] = home[my_row(g, r)]
            xsend[2 * g + r] = (csend[g, r] * scale).astype(BF16)
        joint_row = jnp.where(outer, 1 + g * (rows - 3), 2 + g * (rows - 5))
        xsend[4 + g] = (home[joint_row] * scale).astype(BF16)
    for p in range(rows // 2):
        scaled = jnp.concatenate(
            [(home[2 * p + i] * scale).astype(BF16) for i in range(2)], axis=1
        )
        lifted = dot(liftw[...], scaled)
        for i in range(2):
            feats0[2 * p + i] = modulate(lifted[:, i * lon : (i + 1) * lon], 0, core).astype(BF16)
    pl.semaphore_wait(barrier, n_hor - 1 + n_near * (1 + core))
    even = lax.rem(lat, 2) == 0
    send_order = [(0, even), (1, lat >= 0), (0, jnp.logical_not(even))]
    for side, when in send_order:

        @pl.when(has(side) & when)
        def _():
            first_halo(side, core).start()

    sig_copy.start()
    x_copy.start()
    ret_copy.start()
    cur_copy.start()
    pooled = jnp.zeros((hidden, lon), F32)
    for first in (0, 2):
        flat = [feats0[first + 4 * g + r] for g in range(2) for r in range(2)]
        pooled = pooled + dot(jnp.concatenate(flat, axis=1), poolm[...])
    pooled = packed(pooled)
    qsend[0] = pooled.astype(WIRE)
    psend[0, core] = pooled
    psend[0, other] = jnp.zeros((half, lon), F32)
    send_far_pool(0)
    pool_copy(0).start()
    rate[core] = packed_rate(rets[core])
    for d in range(1, n_chip):
        for to in range(2):

            @pl.when(chip + d < n_chip)
            def _():
                far_rate_copy(d, to, core).start()

    for load in loads[7:]:
        load.wait()
    taps[...] = jnp.concatenate([convw[a] for a in range(3)], axis=1)

    for c in range(2):

        @pl.when(core == c)
        def _():
            row_of = outer_row if c else inner_row
            for g in range(2):
                for r in range(2):
                    place(feats0[row_of(g, r)].astype(F32), c, g, r)
                frecv[0, g, c] = feats0[(2 + g * (rows - 5)) if c else (1 + g * (rows - 3))]
            convolve(c, c, 0)
            remote(sig.at[1 - c], sig.at[1 - c], l_sem.at[2], g_sem.at[0], partner).wait_recv()
            set_modulation(0, 1 - c)
            x_copy.wait_recv()
            for p in range(3):
                got = jnp.concatenate([xrecv[2 * p], xrecv[2 * p + 1]], axis=1)
                lifted = dot(liftw[...], got)
                for i in range(2):
                    feat = modulate(lifted[:, i * lon : (i + 1) * lon], 0, 1 - c)
                    if p < 2:
                        place(feat, 1 - c, p, i)
                    else:
                        frecv[0, i, 1 - c] = feat.astype(BF16)
            convolve(1 - c, c, 0)

    remote(rets.at[other], rets.at[other], l_sem.at[3], g_sem.at[1], partner).wait_recv()
    rate[other] = packed_rate(rets[other])
    remote(csend, cur.at[other], l_sem.at[4], g_sem.at[2], partner).wait_recv()
    for copy in (sig_copy, ret_copy, cur_copy, x_copy):
        copy.wait_send()
    for side in range(2):

        @pl.when(has(side))
        def _():
            first_halo(side, core).wait_send()

    def far_rates():
        for d in range(1, n_chip):

            @pl.when(chip >= d)
            def _():
                for c in range(2):
                    far_rate_copy(d, 0, c).wait_recv()
                second = packed_rate(rfar[d - 1, 1])
                raw_rate[d - 1] = second
                if d < n_chip - 1:
                    pair = packed_rate(rfar[d - 1, 0]) * second
                    coef[d] = pair if d == 1 else coef[d - 1] * pair

    def step(s, final):
        keep, gain, scale_next = [], [], []
        for f in range(2):
            now, after = sig[f, pl.ds(s, 1), :], sig[f, pl.ds(s + 1, 1), :]
            ratio = after / now
            keep.append(ratio + (1.0 - ratio) / (now * now + 1.0))
            gain.append((1.0 - ratio) * (now * in_scale_of(now)))
            scale_next.append(in_scale_of(after))

        if not final:

            @pl.when((s == STEPS - 2) & (chip > 0))
            def _():
                last, end = sig[0, pl.ds(s + 1, 1), :], sig[0, pl.ds(s + 2, 1), :]
                hold = keep[0] * (end / last + (1.0 - end / last) / (last * last + 1.0))
                for g in range(2):
                    for r in range(2):
                        base_send[g, r, 0:chans, :] = (hold * cur[0, g, r]).astype(BF16)
                base_copy(core).start()

        def await_feats():
            @pl.when(s > 0)
            def _():
                feat_copy(s).wait_recv()

        def joint_edges(c):
            for g in range(2):
                j = joint(g, c)
                rhs = [shifted(frecv[s, g, f].astype(F32)) for f in range(2)]
                extra = dot(convw[2 * j], jnp.concatenate(rhs, axis=1))
                for f in range(2):
                    acc[f][g, j] += extra[:, f * lon : (f + 1) * lon]

        def await_halos():
            for side in range(2):
                if not final:

                    @pl.when(has(side) & (s == 0))
                    def _():
                        for f in range(2):
                            first_halo(1 - side, f).wait_recv()

                @pl.when(has(side) & (s > 0))
                def _():
                    halo_copy(s, 1 - side).wait_recv()

        def remote_edges(frames):
            near = [hrecv[s, side, f, 0:chans, :] for side in range(2) for f in frames]
            near = dot(liftw[...], jnp.concatenate(near, axis=1))
            for side in range(2):
                rhs = []
                for i, f in enumerate(frames):
                    at = (side * len(frames) + i) * lon
                    feat = modulate(near[:, at : at + lon], s, f)
                    rhs.append(shifted(jnp.where(has(side), feat, 0.0)))
                extra = dot(convw[2 * side], jnp.concatenate(rhs, axis=1))
                for i, f in enumerate(frames):
                    acc[f][side, side] += extra[:, i * lon : (i + 1) * lon]

        def await_pools():
            if not final:

                @pl.when(s == 0)
                def _():
                    far_rates()

            pool_copy(s).wait_recv()
            for d in range(1, n_chip):
                for c in range(2):

                    @pl.when(chip >= d)
                    def _():
                        far_pool_wait(s, d, c).wait_recv()

        def contexts():
            first = psend[s, 0] + precv[s, 0]
            if n_chip > 1:
                total = jnp.zeros((half, lon), F32)
                for d in range(1, n_chip):
                    got = qrecv[s, d - 1, 0].astype(F32)
                    if not final:
                        got = got * jnp.where(s == 0, raw_rate[d - 1], 1.0)
                    got = got + qrecv[s, d - 1, 1].astype(F32)
                    got = got if d == 1 else coef[d - 1] * got
                    total = total + jnp.where(chip >= d, got, 0.0)
                first = first + rate[0] * total
            second = rate[1] * first + (psend[s, 1] + precv[s, 1])
            both = []
            for total in (first, second):
                high = total.astype(BF16)
                both.append(jnp.concatenate([high, (total - high.astype(F32)).astype(BF16)], axis=1))
            both = jnp.concatenate(both, axis=0)
            for side in range(2):
                wide = dot(both, spread[side])
                for f in range(2):
                    for tok in range(2):
                        up[f, tok, side * half : (side + 1) * half, :] = wide[
                            f * half : (f + 1) * half, tok * lon : (tok + 1) * lon
                        ]

        def finish(cells):
            gated = []
            for f, g, r in cells:
                feat = feature(f, g, r).astype(F32)
                gated.append(half_silu(0.5 * (feat + acc[f][g, r] + up[f, g])).astype(BF16))
            outputs = dot(outw[...], jnp.concatenate(gated, axis=1))
            for i, (f, g, r) in enumerate(cells):
                nxt = keep[f] * cur[f, g, r] + gain[f] * outputs[:, i * lon : (i + 1) * lon]
                cur[f, g, r] = nxt
                if g == r and not final:
                    hsend[s + 1, g, f, 0:chans, :] = (nxt * scale_next[f]).astype(BF16)
                if f == 0 and final:
                    rest_send[1 if g == r else 0, g, 0:chans, :] = (
                        nxt - base_send[g, r, 0:chans, :].astype(F32)
                    ).astype(BF16)

        def send_rest(copy):
            @pl.when(chip > 0)
            def _():
                copy.start()

        def lift(pairs):
            for pair in pairs:
                f = pair[0][0]
                scaled = jnp.concatenate(
                    [(cur[cell] * scale_next[f]).astype(BF16) for cell in pair], axis=1
                )
                lifted = dot(liftw[...], scaled)
                for i, cell in enumerate(pair):
                    place(modulate(lifted[:, i * lon : (i + 1) * lon], s + 1, f), *cell)

        def send_feats(c):
            @pl.when(s > 0)
            def _():
                feat_copy(s).wait_send()

            for f in range(2):
                for g in range(2):
                    fsend[s + 1, g, f] = feature(f, g, joint(g, c))
            feat_copy(s + 1).start()

        def send_pools():
            pooled = None
            for cells in (near_cells, edge_cells):
                flat = [jnp.concatenate([feature(*cell) for cell in cells[f]], axis=1) for f in range(2)]
                part = dot(jnp.concatenate(flat, axis=0), poolm[lon : 3 * lon, :])
                pooled = part if pooled is None else pooled + part
            first, second = (packed(pooled[f * hidden : (f + 1) * hidden]) for f in range(2))
            qsend[s + 1] = (rate[1] * first + second).astype(WIRE)
            drain_far_pool(s)
            send_far_pool(s + 1)
            psend[s + 1, 0] = first
            psend[s + 1, 1] = second
            pool_copy(s).wait_send()
            pool_copy(s + 1).start()

        near_cells = [[(f, 0, 1), (f, 1, 0)] for f in range(2)]
        edge_cells = [[(f, 0, 0), (f, 1, 1)] for f in range(2)]

        def send_edges():
            for side, when in send_order:

                @pl.when(has(side) & when & (s > 0))
                def _():
                    halo_copy(s, side).wait_send()

                @pl.when(has(side) & when)
                def _():
                    halo_copy(s + 1, side).start()

        all_near, all_edge = near_cells[0] + near_cells[1], edge_cells[0] + edge_cells[1]

        def lift_near():
            for f in range(2):
                set_modulation(s + 1, f)
            lift(near_cells)
            send_feats(1)

        @pl.when(outer)
        def _():
            await_pools()
            contexts()
            finish(all_near)
            if final:
                send_rest(outer_rest(0))

            if not final:

                @pl.when(chip == 0)
                def _():
                    lift_near()

            await_halos()
            remote_edges([0, 1])
            finish(all_edge)
            if final:
                send_rest(outer_rest(1))
                feat_copy(s).wait_send()
            else:
                send_edges()

            if final:
                for f in range(2):
                    final_copy(f).start()
            else:

                @pl.when(chip > 0)
                def _():
                    lift_near()

                lift(edge_cells)
                send_pools()
                feat_copy(s + 1).wait_recv()
                for f in range(2):
                    convolve(f, 1, s + 1)

        @pl.when(jnp.logical_not(outer))
        def _():
            await_feats()
            joint_edges(0)
            await_pools()
            contexts()
            if final:
                finish(near_cells[0] + edge_cells[0])
                send_rest(inner_rest)
                feat_copy(s).wait_send()
                finish(near_cells[1] + edge_cells[1])
                final_copy(1).start()
            else:
                finish(near_cells[0] + edge_cells[0])
                finish(near_cells[1] + edge_cells[1])
                for f in range(2):
                    set_modulation(s + 1, f)
                lift(edge_cells)
                send_feats(0)
                lift(near_cells)
                send_pools()
                for f in range(2):
                    convolve(f, 0, s + 1)

    for s in range(STEPS - 1):
        step(s, False)

    step(STEPS - 1, True)

    def put(out, row, value):
        out[pl.ds(row, chans, stride=rows), :] = value

    cells = [(g, r) for g in range(2) for r in range(2)]

    @pl.when(outer)
    def _():
        for g, r in cells:
            put(wout, outer_row(g, r), cur[1, g, r])

        final_copy(1).wait_recv()
        for g, r in cells:
            put(wout, inner_row(g, r), fin_recv[1, g, r])

        @pl.when(chip == n_chip - 1)
        def _():
            fresh_load.wait()
            arr[...] = plan[plan.shape[0] - 1] * arr[...]

        @pl.when(chip < n_chip - 1)
        def _():
            for c in range(2):
                base_copy(c).wait_recv()
            inner_rest.wait_recv()
            for c, stage in ((0, 0), (0, 1), (1, 0), (1, 1)):
                if c:
                    outer_rest(stage).wait_recv()
                for g in range(2):
                    r = g if stage else 1 - g
                    row = outer_row(g, r) if c else inner_row(g, r)
                    value = base_recv[c, g, r, 0:chans, :].astype(F32)
                    put(arr, row, value + rest_recv[c, stage, g, 0:chans, :].astype(F32))

    @pl.when(jnp.logical_not(outer))
    def _():
        for g, r in cells:
            put(wout, inner_row(g, r), cur[0, g, r])
            put(arr, inner_row(g, r), cur[1, g, r])
        for f, out in ((1, arr), (0, wout)):
            final_copy(f).wait_recv()
            for g, r in cells:
                put(out, outer_row(g, r), fin_recv[f, g, r])

    final_copy(1).wait_send()
    pool_copy(STEPS - 1).wait_send()
    drain_far_pool(STEPS - 1)
    for d in range(1, n_chip):
        for to in range(2):

            @pl.when(chip + d < n_chip)
            def _():
                far_rate_copy(d, to, core).wait_send()

    for side in range(2):

        @pl.when(outer & has(side))
        def _():
            halo_copy(STEPS - 1, side).wait_send()

    @pl.when(outer)
    def _():
        final_copy(0).wait_send()

    @pl.when(chip > 0)
    def _():
        base_copy(core).wait_send()

    @pl.when((chip > 0) & outer)
    def _():
        for stage in range(2):
            outer_rest(stage).wait_send()

    @pl.when((chip > 0) & jnp.logical_not(outer))
    def _():
        inner_rest.wait_send()


def write(a, b, a_out, b_out, sem):
    copies = [pltpu.make_async_copy(x, y, sem.at[i]) for i, (x, y) in enumerate([(a, a_out), (b, b_out)])]
    for copy in copies:
        copy.start()
    for copy in copies:
        copy.wait()


def body(
    n_hor,
    n_lat,
    window,
    fresh_noise,
    level_index,
    plan,
    retention,
    lift_weight,
    mod_scale,
    mod_shift,
    conv_weight,
    out_weight,
):
    frames, chans, rows, lon = window.shape
    hidden = conv_weight.shape[1]
    half = hidden // 2
    cpad = -(-chans // 8) * 8
    n_chip = n_hor // 2
    peers = max(1, n_chip - 1)
    vmem = pl.BlockSpec(memory_space=pltpu.VMEM)
    hbm = pl.BlockSpec(memory_space=pltpu.HBM)
    flat = jax.ShapeDtypeStruct((chans * rows, lon), F32)
    dma = pltpu.SemaphoreType.DMA
    current, arriving = pl.pallas_call(
        functools.partial(kernel, rows, lon, n_hor, n_lat),
        out_shape=(pltpu.VMEM(flat.shape, F32), pltpu.VMEM(flat.shape, F32)),
        in_specs=[hbm] * 10,
        out_specs=(vmem, vmem),
        scratch_shapes=[
            pltpu.SMEM(level_index.shape, jnp.int32),
            pltpu.SMEM(plan.shape, F32),
            pltpu.VMEM((chans * rows, lon), F32),
            pltpu.VMEM((2, 1, hidden), F32),
            pltpu.VMEM((peers, 2, 1, hidden), F32),
            pltpu.VMEM((1, hidden), F32),
            pltpu.VMEM((1, hidden), F32),
            pltpu.VMEM((chans, hidden), BF16),
            pltpu.VMEM(conv_weight.shape, BF16),
            pltpu.VMEM((chans, hidden), BF16),
            pltpu.VMEM((hidden, chans), BF16),
            pltpu.VMEM((hidden, 9 * hidden), BF16),
            pltpu.VMEM((rows, chans, lon), F32),
            pltpu.VMEM((rows, hidden, lon), BF16),
            pltpu.VMEM((2, 2, chans, lon), F32),
            pltpu.VMEM((6, chans, lon), BF16),
            pltpu.VMEM((6, chans, lon), BF16),
            pltpu.VMEM((2, 2, 2, chans, lon), F32),
            pltpu.VMEM((8, 3 * hidden, lon), BF16),
            pltpu.VMEM((8, 3 * hidden, lon), BF16),
            pltpu.VMEM((STEPS, 2, 2, hidden, lon), BF16),
            pltpu.VMEM((STEPS, 2, 2, hidden, lon), BF16),
            pltpu.VMEM((2, 2, hidden, lon), F32),
            pltpu.VMEM((2, 2, hidden, lon), F32),
            pltpu.VMEM((2, 2, hidden, lon), F32),
            pltpu.VMEM((2, hidden, lon), F32),
            pltpu.VMEM((2, 2, 2, hidden, lon), F32),
            pltpu.VMEM((2, 8, lon), F32),
            pltpu.VMEM((4 * lon, lon), BF16),
            pltpu.VMEM((2, 2 * lon, 2 * lon), BF16),
            pltpu.VMEM((2, half, lon), F32),
            pltpu.VMEM((peers, half, lon), F32),
            pltpu.VMEM((peers, half, lon), F32),
            pltpu.VMEM((STEPS + 1, 2, 2, cpad, lon), BF16),
            pltpu.VMEM((STEPS, 2, 2, cpad, lon), BF16),
            pltpu.VMEM((STEPS, 2, half, lon), F32),
            pltpu.VMEM((STEPS, 2, half, lon), F32),
            pltpu.VMEM((STEPS, half, lon), WIRE),
            pltpu.VMEM((STEPS, peers, 2, half, lon), WIRE),
            pltpu.VMEM((2, 2, cpad, lon), BF16),
            pltpu.VMEM((2, 2, 2, cpad, lon), BF16),
            pltpu.VMEM((2, 2, cpad, lon), BF16),
            pltpu.VMEM((2, 2, 2, cpad, lon), BF16),
            pltpu.VMEM((2, 2, 2, chans, lon), F32),
            dma((10,)),
            dma((4,)),
            dma((3, 2)),
            dma((2,)),
            dma((3,)),
            dma((peers, 2)),
            dma((STEPS, peers, 2)),
            dma((peers, 2)),
            dma((peers, 2)),
            dma((5,)),
            dma((2,)),
        ],
        compiler_params=pltpu.CompilerParams(
            collective_id=0, has_side_effects=True, vmem_limit_bytes=66400000
        ),
    )(
        level_index,
        plan,
        window.reshape(chans * rows, lon),
        fresh_noise.reshape(chans * rows, lon),
        retention,
        mod_scale.reshape(1, hidden),
        mod_shift.reshape(1, hidden),
        lift_weight.T,
        conv_weight,
        out_weight,
    )
    shape = (frames, chans, rows, lon)
    current, rolled = pl.pallas_call(
        write,
        out_shape=(flat, flat),
        in_specs=[vmem, vmem],
        out_specs=(hbm, hbm),
        scratch_shapes=[dma((2,))],
        compiler_params=pltpu.CompilerParams(vmem_limit_bytes=4 * 1024 * 1024),
    )(current, arriving)
    return (current.reshape(shape), rolled.reshape(shape))


def solution(mesh):
    in_specs = (
        P("hor", None, "lat", None),
        P(None, "lat", None),
        P("hor"),
        P(),
        P("hor", None),
        P(),
        P(),
        P(),
        P(),
        P(),
    )
    out_specs = (P("hor", None, "lat", None), P("hor", None, "lat", None))
    run = functools.partial(body, mesh.shape["hor"], mesh.shape["lat"])
    return jax.shard_map(run, mesh=mesh, in_specs=in_specs, out_specs=out_specs, check_vma=False)
```
